32 devices in a mesh: group: 2 (over x), gx: 16 (over z, y, core).
Axes of the slice: x: 2, y: 2, z: 4, core: 2. Of those that a mesh axis runs over, the one named last changes fastest.
Arguments:
- features: bfloat16 [192, 256, 16, 128], P(('group', 'gx')), parts along dimension 0, may hold values from -6 to 6
- occupancy: int32 [192, 256, 16], P(('group', 'gx')), parts along dimension 0, may hold values from 0 to 3
- heights: int32 [192, 256], P(('group', 'gx')), parts along dimension 0, may hold values from 0 to 16, as said below
- xy_in: bfloat16 [128, 512], replicated, may hold values from -0.5 to 0.5
- xy_out: bfloat16 [512, 128], replicated, may hold values from -0.25 to 0.25
- xz_in: bfloat16 [128, 512], replicated, may hold values from -0.5 to 0.5
- xz_out: bfloat16 [512, 128], replicated, may hold values from -0.25 to 0.25
- yz_in: bfloat16 [128, 512], replicated, may hold values from -0.5 to 0.5
- yz_out: bfloat16 [512, 128], replicated, may hold values from -0.25 to 0.25
- voxel_in: bfloat16 [128, 256], replicated, may hold values from -0.5 to 0.5
- voxel_out: bfloat16 [256, 128], replicated, may hold values from -0.375 to 0.375
Outputs:
- encoded: bfloat16 [192, 256, 16, 128], P(('group', 'gx')), parts along dimension 0
The draws below stay inside these ranges and needn't reach their ends.
There are 2 independent parts, one for each index of `group`. The reference program is written for one: setup_inputs(seed, part) draws one part's arguments, and reference() takes and returns one part's arrays. A program takes and returns all parts, laid end to end along the dimension named above; an argument that names none is the same for every part. Nothing has to cross between parts.
Inputs may be any that keep to these rules, and one draw needn't show every extreme that they name: `heights`: cells of a column with height index below its valid height count.
All inputs are finite; a program needn't handle non-finite values.
Results may differ from the reference program's by a relative error of at most 0.0073.
Values may be sent and summed in bfloat16 or wider, within the bound.
No kernel may reach another device: no remote copies, remote signals or barrier semaphores. Data moves between devices by JAX's collectives and lax.ppermute only.
A program may use at most 64 MiB of HBM per device.

```python
import jax
import jax.numpy as jnp
from jax import lax

Y = 256
Z = 16
C = 128
PH = 512
VH = 256
X = 96


def draw_heights(key, part):
    lowest = max(Z // 3, 1)
    xs = jnp.arange(X, dtype=jnp.int32)
    ceiling = lowest + (Z - lowest) * xs // (X - 1)
    raw = jax.random.randint(key, (X, Y), 0, 1 << 20)
    height = raw % (ceiling[:, None] + 1)
    height = height.at[X - 1, 0].set(Z).at[0, 0].set(0)
    return height.astype(jnp.int32)


def set_ends(array, rng, smallest, largest):
    longest = array.shape.index(max(array.shape))
    spots = []
    for shift in (0, 1):
        where = [jax.random.randint(jax.random.fold_in(rng, axis), (), 0, length) for axis, length in enumerate(array.shape)]
        where[longest] = (where[longest] + shift) % array.shape[longest]
        spots.append(tuple(where))
    return array.at[spots[0]].set(smallest).at[spots[1]].set(largest)


def raised(result, own_key, source, target, parts, factor):
    def block_of(axis_at):
        return (jnp.arange(result.shape[axis_at]) // (result.shape[axis_at] // parts)).reshape((-1,) + (1,) * (result.ndim - 1 - axis_at))

    near = jax.random.permutation(own_key, parts)[block_of(target)]
    second = (block_of(target) + parts // 2) % parts
    return jnp.where((block_of(source) == near) | (block_of(source) == second), factor * result, result)


def shard_levels(rng, shape, split, low, largest):
    level = 1.0
    for position, blocks in split:
        draws = jax.random.uniform(jax.random.fold_in(jax.random.fold_in(rng, 6), position), (blocks,), jnp.float32, low / len(split), largest / len(split))
        level = level * jnp.repeat(jnp.exp(draws), shape[position] // blocks).reshape((-1,) + (1,) * (len(shape) - 1 - position))
    return level


def normal_values(stream_key, shape, scale, most, split=(), held_as=jnp.bfloat16):
    entries = scale * jax.random.normal(stream_key, shape, jnp.float32)
    if split:
        entries = entries * shard_levels(stream_key, shape, split, -0.22, 0.18)
    return jnp.clip(entries, -most, most).astype(held_as)


def gaussian_with(key, shape, deviation, reach, cuts, heavy, kind=jnp.bfloat16):
    drawn = deviation * jax.random.normal(key, shape, jnp.float32)
    if cuts:
        drawn = drawn * shard_levels(key, shape, cuts, -0.22, 0.18)
    return jnp.clip(raised(drawn, jax.random.fold_in(key, 3), *heavy), -reach, reach).astype(kind)


def setup_inputs(seed: int = 0, part: int = 0) -> dict:
    seeds = jax.random.split(jax.random.key(seed), 12)
    part_keys = jax.random.split(jax.random.fold_in(seeds[11], part), 12)
    return {
        "features": gaussian_with(part_keys[0], (X, Y, Z, C), 1.0, 6.0, ((0, 16),), (0, 1, 16, 2.0)),
        "occupancy": set_ends(jax.random.randint(part_keys[1], (X, Y, Z), 0, 4), jax.random.fold_in(part_keys[1], 1), 0, 3).astype(jnp.int32),
        "heights": draw_heights(jax.random.fold_in(jax.random.fold_in(seeds[11], part), 71), part),
        "xy_in": normal_values(seeds[3], (C, PH), C ** -0.5, 0.5),
        "xy_out": normal_values(seeds[4], (PH, C), PH ** -0.5, 0.25),
        "xz_in": normal_values(seeds[5], (C, PH), C ** -0.5, 0.5),
        "xz_out": normal_values(seeds[6], (PH, C), PH ** -0.5, 0.25),
        "yz_in": normal_values(seeds[7], (C, PH), C ** -0.5, 0.5),
        "yz_out": normal_values(seeds[8], (PH, C), PH ** -0.5, 0.25),
        "voxel_in": normal_values(seeds[9], (C, VH), C ** -0.5, 0.5),
        "voxel_out": normal_values(seeds[10], (VH, C), VH ** -0.5, 0.375),
    }


def plane_mlp(pool, w_in, w_out):
    hidden = jax.nn.silu(jnp.dot(pool, w_in, preferred_element_type=jnp.float32)).astype(jnp.bfloat16)
    return jnp.dot(hidden, w_out, preferred_element_type=jnp.float32).astype(jnp.bfloat16)

def reference(features, occupancy, heights, xy_in, xy_out, xz_in, xz_out, yz_in, yz_out, voxel_in, voxel_out):
    zidx = jnp.arange(Z, dtype=jnp.int32)

    def one_row(carry, item):
        feat, occ, hgt = item
        valid = (zidx[None, :] < hgt[:, None]).astype(jnp.int32)
        weight = (occ * valid).astype(jnp.float32)
        wide = feat.astype(jnp.float32)
        xy_sum = jnp.einsum('yz,yzc->yc', weight, wide)
        xy_pool = xy_sum / jnp.sqrt(1.0 + lax.optimization_barrier(jnp.sum(weight, axis=1)))[:, None]
        xz_sum = jnp.einsum('yz,yzc->zc', weight, wide)
        xz_pool = xz_sum / jnp.sqrt(1.0 + lax.optimization_barrier(jnp.sum(weight, axis=0)))[:, None]
        total, count = carry
        return ((total + weight[:, :, None] * wide, count + weight), (xy_pool.astype(jnp.bfloat16), xz_pool.astype(jnp.bfloat16)))
    init = (jnp.zeros((Y, Z, C), jnp.float32), jnp.zeros((Y, Z), jnp.float32))
    (total, count), (xy_pool, xz_pool) = lax.scan(one_row, init, (features, occupancy, heights))
    yz_pool = (total / jnp.sqrt(1.0 + count)[:, :, None]).astype(jnp.bfloat16)
    xy_plane = plane_mlp(xy_pool.reshape(X * Y, C), xy_in, xy_out).reshape(X, Y, C)
    xz_plane = plane_mlp(xz_pool.reshape(X * Z, C), xz_in, xz_out).reshape(X, Z, C)
    yz_plane = plane_mlp(yz_pool.reshape(Y * Z, C), yz_in, yz_out).reshape(Y, Z, C)

    def voxel_row(item):
        feat, xy_row, xz_row = item
        mixed = feat.astype(jnp.float32) + xy_row[:, None, :].astype(jnp.float32) + xz_row[None, :, :].astype(jnp.float32) + yz_plane.astype(jnp.float32)
        mixed = mixed.astype(jnp.bfloat16).reshape(Y * Z, C)
        return plane_mlp(mixed, voxel_in, voxel_out).reshape(Y, Z, C)
    return lax.map(voxel_row, (features, xy_plane, xz_plane))
```

```python
import functools

import jax
import jax.numpy as jnp
from jax import lax
from jax.experimental import pallas as pl
from jax.experimental.pallas import tpu as pltpu
from jax.sharding import PartitionSpec as P


BF = jnp.bfloat16
F32 = jnp.float32


def radices(n):
    digits, left = [2], n // 2
    while left > 1:
        digits.append(4 if left % 4 == 0 else 2)
        left //= digits[-1]
    return digits


def offsets(n):
    table, weight = [0], 1
    for digit in radices(n):
        table = [base + d * weight for base in table for d in range(digit)]
        weight *= digit
    return table


def silu(half):
    return half + half * jnp.tanh(half)


def mlp(x, w_in, w_out):
    hidden = silu(0.5 * jnp.dot(x, w_in, preferred_element_type=F32)).astype(BF)
    return jnp.dot(hidden, w_out, preferred_element_type=F32).astype(BF)


def pool_body(pos_ref, feat_ref, occ_ref, hgt_ref, part_ref, xy_ref, xz_ref, xz_acc, xz_cnt):
    step = pl.program_id(0)
    rows, ys, zs, chans = feat_ref.shape
    y_len = occ_ref.shape[2]

    @pl.when(step == 0)
    def _():
        xz_acc[...] = jnp.zeros_like(xz_acc)
        xz_cnt[...] = jnp.zeros_like(xz_cnt)

    zidx = lax.broadcasted_iota(jnp.int32, (zs, y_len), 0)
    lane = lax.broadcasted_iota(jnp.int32, (zs, y_len), 1)
    mine = lane < ys
    shift = lax.rem(y_len - step * ys, y_len)
    sums = [None] * ys
    count = None
    for x in range(rows):
        weight = jnp.where(zidx < hgt_ref[x : x + 1, :], occ_ref[x], 0).astype(F32)
        weight = pltpu.roll(weight, shift, 1)
        weight = jnp.where(mine, weight, 0.0)
        count = weight if count is None else count + weight
        xz_cnt[x] += weight
        xy_scale = lax.rsqrt(1.0 + jnp.sum(weight, axis=0, keepdims=True))
        acc = xz_acc[x]
        xy_rows = []
        for y in range(ys):
            g = feat_ref[x, y].astype(F32) * jnp.broadcast_to(weight[:, y : y + 1], (zs, chans))
            sums[y] = g if sums[y] is None else sums[y] + g
            acc = acc + g
            total = jnp.sum(g, axis=0, keepdims=True)
            xy_rows.append(total * jnp.broadcast_to(xy_scale[:, y : y + 1], (1, chans)))
        xz_acc[x] = acc
        xy_ref[0, x] = jnp.concatenate(xy_rows, axis=0).astype(BF)
    for y in range(ys):
        part_ref[0, y * zs : (y + 1) * zs, :] = sums[y].astype(BF)
    part_ref[0, ys * zs :, :] = count[:, :chans].astype(BF)

    @pl.when(step == pl.num_programs(0) - 1)
    def _():
        for x in range(rows):
            scale = lax.rsqrt(1.0 + jnp.sum(xz_cnt[x], axis=1, keepdims=True))
            xz_ref[x] = (xz_acc[x] * jnp.broadcast_to(scale, (zs, chans))).astype(BF)


def pools(feat, occ, hgt, me, n):
    rows, y_len, zs, chans = feat.shape
    ys = y_len // n
    table = offsets(n)
    place = [0] * n
    for pos, off in enumerate(table):
        place[off] = pos
    where = jnp.asarray(place, jnp.int32)[jnp.arange(n, dtype=jnp.int32) ^ me]
    grid_spec = pltpu.PrefetchScalarGridSpec(
        num_scalar_prefetch=1,
        grid=(n,),
        in_specs=[
            pl.BlockSpec((rows, ys, zs, chans), lambda i, w: (0, i, 0, 0)),
            pl.BlockSpec((rows, zs, y_len), lambda i, w: (0, 0, 0)),
            pl.BlockSpec((rows, y_len), lambda i, w: (0, 0)),
        ],
        out_specs=[
            pl.BlockSpec((1, ys * zs + zs, chans), lambda i, w: (w[i], 0, 0)),
            pl.BlockSpec((1, rows, ys, chans), lambda i, w: (i, 0, 0, 0)),
            pl.BlockSpec((rows, zs, chans), lambda i, w: (0, 0, 0)),
        ],
        scratch_shapes=[pltpu.VMEM((rows, zs, chans), F32), pltpu.VMEM((rows, zs, y_len), F32)],
    )
    return pl.pallas_call(
        pool_body,
        grid_spec=grid_spec,
        out_shape=[
            jax.ShapeDtypeStruct((n, ys * zs + zs, chans), BF),
            jax.ShapeDtypeStruct((n, rows, ys, chans), BF),
            jax.ShapeDtypeStruct((rows, zs, chans), BF),
        ],
        compiler_params=pltpu.CompilerParams(vmem_limit_bytes=24 << 20),
        cost_estimate=pl.CostEstimate(flops=8 * feat.size, bytes_accessed=2 * feat.size, transcendentals=0),
        name="pools",
    )(where, pltpu.with_memory_space_constraint(feat, pltpu.MemorySpace.HBM), occ, hgt)


def planes_body(xy_ref, xz_ref, xy_in, xy_out, xz_in, xz_out, xy_plane, xz_plane):
    size = min(256, xy_ref.shape[0])
    for r in range(0, xy_ref.shape[0], size):
        xy_plane[r : r + size] = mlp(xy_ref[r : r + size], xy_in[...], xy_out[...])
    xz_plane[...] = mlp(xz_ref[...], xz_in[...], xz_out[...])


def planes(xy_pool, xz_pool, xy_in, xy_out, xz_in, xz_out):
    vmem = pl.BlockSpec(memory_space=pltpu.VMEM)
    flops = 4 * (xy_pool.size + xz_pool.size) * xy_in.shape[1]
    return pl.pallas_call(
        planes_body,
        in_specs=[vmem] * 6,
        out_specs=[vmem] * 2,
        out_shape=[jax.ShapeDtypeStruct(xy_pool.shape, BF), jax.ShapeDtypeStruct(xz_pool.shape, BF)],
        compiler_params=pltpu.CompilerParams(vmem_limit_bytes=16 << 20),
        cost_estimate=pl.CostEstimate(flops=flops, bytes_accessed=1 << 20, transcendentals=0),
        name="planes",
    )(xy_pool, xz_pool, xy_in, xy_out, xz_in, xz_out)


def yz_body(parts, zs, *refs):
    w_in, w_out, out = refs[parts:]
    total = refs[0][...].astype(F32)
    for ref in refs[1:parts]:
        total = total + ref[...].astype(F32)
    cells, chans = out.shape
    scale = lax.rsqrt(1.0 + total[cells:])
    pool = [
        total[r : r + zs] * jnp.broadcast_to(scale[:, y : y + 1], (zs, chans))
        for y, r in enumerate(range(0, cells, zs))
    ]
    out[...] = mlp(jnp.concatenate(pool, axis=0).astype(BF), w_in[...], w_out[...])


def yz_mlp(parts, zs, w_in, w_out):
    vmem = pl.BlockSpec(memory_space=pltpu.VMEM)
    cells, chans = parts[0].shape[0] - zs, parts[0].shape[1]
    return pl.pallas_call(
        functools.partial(yz_body, len(parts), zs),
        in_specs=[vmem] * (len(parts) + 2),
        out_specs=vmem,
        out_shape=jax.ShapeDtypeStruct((cells, chans), BF),
        compiler_params=pltpu.CompilerParams(vmem_limit_bytes=16 << 20),
        cost_estimate=pl.CostEstimate(flops=4 * cells * w_in.size, bytes_accessed=1 << 19, transcendentals=0),
        name="yz_mlp",
    )(*parts, w_in, w_out)


def voxel_body(which, feat_ref, xy_ref, xz_ref, yz_ref, w_in, w_out, out_ref):
    rows, ys, zs, chans = feat_ref.shape
    yz = yz_ref[0].astype(F32)
    for x in range(rows):
        xy = xy_ref[0, x].astype(F32)
        xz = xz_ref[x].astype(F32)
        mixed = feat_ref[x].astype(F32) + xy[:, None, :] + xz[None, :, :]
        mixed = (mixed.reshape(ys * zs, chans) + yz).astype(BF)
        out_ref[x] = mlp(mixed, w_in[...], w_out[...]).reshape(ys, zs, chans)


def voxels(feat, xy_plane, xz_plane, yz_plane, w_in, w_out, me, n):
    rows, y_len, zs, chans = feat.shape
    ys = y_len // n
    which = jnp.asarray(offsets(n), jnp.int32) ^ me
    whole = lambda a: pl.BlockSpec(a.shape, lambda i, w: (0,) * a.ndim)
    grid_spec = pltpu.PrefetchScalarGridSpec(
        num_scalar_prefetch=1,
        grid=(n,),
        in_specs=[
            pl.BlockSpec((rows, ys, zs, chans), lambda i, w: (0, w[i], 0, 0)),
            pl.BlockSpec((1, rows, ys, chans), lambda i, w: (w[i], 0, 0, 0)),
            whole(xz_plane),
            pl.BlockSpec((1, ys * zs, chans), lambda i, w: (i, 0, 0)),
            whole(w_in),
            whole(w_out),
        ],
        out_specs=pl.BlockSpec((rows, ys, zs, chans), lambda i, w: (0, w[i], 0, 0)),
    )
    return pl.pallas_call(
        voxel_body,
        grid_spec=grid_spec,
        out_shape=jax.ShapeDtypeStruct(feat.shape, BF),
        compiler_params=pltpu.CompilerParams(vmem_limit_bytes=24 << 20),
        cost_estimate=pl.CostEstimate(
            flops=4 * feat.size * w_in.shape[1], bytes_accessed=4 * feat.size, transcendentals=0
        ),
        name="voxels",
    )(which, feat, xy_plane, xz_plane, yz_plane, w_in, w_out)


def swap(value, n, offset):
    return lax.ppermute(value, "gx", [(i, i ^ offset) for i in range(n)])


def per_device(n, features, occupancy, heights, xy_in, xy_out, xz_in, xz_out, yz_in, yz_out, voxel_in, voxel_out):
    zs = features.shape[2]
    me = lax.axis_index("gx")
    parts, xy_pool, xz_pool = pools(features, jnp.swapaxes(occupancy, 1, 2), heights, me, n)
    chans = features.shape[3]
    xy_plane, xz_plane = planes(
        xy_pool.reshape(-1, chans), xz_pool.reshape(-1, chans), xy_in, xy_out, xz_in, xz_out
    )
    xy_plane, xz_plane = xy_plane.reshape(xy_pool.shape), xz_plane.reshape(xz_pool.shape)

    digits = radices(n)
    weights = [1]
    for digit in digits:
        weights.append(weights[-1] * digit)
    held = parts
    pieces = None
    for stage, digit in enumerate(digits):
        size = held.shape[0] // digit
        pieces = [held[:size]] + [
            swap(held[d * size : (d + 1) * size], n, d * weights[stage]) for d in range(1, digit)
        ]
        if stage < len(digits) - 1:
            held = sum(piece.astype(F32) for piece in pieces).astype(BF)
    plane = yz_mlp([piece[0] for piece in pieces], zs, yz_in, yz_out)[None]
    for stage, digit in reversed(list(enumerate(digits))):
        plane = jnp.concatenate([plane] + [swap(plane, n, d * weights[stage]) for d in range(1, digit)], axis=0)
    return voxels(features, xy_plane, xz_plane, plane, voxel_in, voxel_out, me, n)


def solution(mesh):
    split = ("group", "gx")
    in_specs = (P(split, None, None, None), P(split, None, None), P(split, None)) + (P(),) * 8
    return jax.shard_map(
        functools.partial(per_device, mesh.shape["gx"]),
        mesh=mesh,
        in_specs=in_specs,
        out_specs=P(split, None, None, None),
        check_vma=False,
    )
```

```python
import functools

import jax
import jax.numpy as jnp
from jax import lax
from jax.experimental import pallas as pl
from jax.experimental.pallas import tpu as pltpu
from jax.sharding import PartitionSpec as P


BF = jnp.bfloat16
F32 = jnp.float32


def radices(n):
    digits, left = [2], n // 2
    while left > 1:
        digits.append(4 if left % 4 == 0 else 2)
        left //= digits[-1]
    return digits


def offset(pos, n):
    off, slower, weight = 0, n, 1
    for digit in radices(n):
        slower //= digit
        off = off + ((pos // slower) % digit) * weight
        weight *= digit
    return off


def silu(half):
    return half + half * jnp.tanh(half)


def mlp(x, w_in, w_out):
    hidden = silu(jnp.dot(x, w_in, preferred_element_type=F32)).astype(BF)
    return jnp.dot(hidden, w_out, preferred_element_type=F32).astype(BF)


def position(off, n):
    pos, slower, weight = 0, n, 1
    for digit in radices(n):
        slower //= digit
        pos = pos + ((off // weight) % digit) * slower
        weight *= digit
    return pos


def pool_body(me_ref, feat_ref, occ_ref, hgt_ref, part_ref, xy_ref, xz_ref, xz_acc, xz_cnt, spread, same_z, same_y):
    step = pl.program_id(0)
    rows, ys, zs, chans = feat_ref.shape
    cells, lanes = ys * zs, occ_ref.shape[2]

    @pl.when(step == 0)
    def _():
        xz_acc[...] = jnp.zeros_like(xz_acc)
        xz_cnt[...] = jnp.zeros_like(xz_cnt)
        y_of = lax.broadcasted_iota(jnp.int32, (lanes, cells), 1) // zs
        spread[...] = (lax.broadcasted_iota(jnp.int32, (lanes, cells), 0) == y_of).astype(F32).astype(BF)
        z_of = lax.broadcasted_iota(jnp.int32, (zs, cells), 1) % zs
        same_z[...] = (lax.broadcasted_iota(jnp.int32, (zs, cells), 0) == z_of).astype(F32)
        y_of = lax.broadcasted_iota(jnp.int32, (ys, cells), 1) // zs
        same_y[...] = (lax.broadcasted_iota(jnp.int32, (ys, cells), 0) == y_of).astype(F32)

    zidx = lax.broadcasted_iota(jnp.int32, (zs, lanes), 0)
    shift = lax.rem(lanes - lax.rem(step * ys, lanes), lanes)
    weights = []
    for x in range(rows):
        weight = jnp.where(zidx < hgt_ref[x : x + 1, :], occ_ref[x], 0).astype(F32)
        weights.append(pltpu.roll(weight, shift, 1))
    count = weights[0]
    for x in range(1, rows):
        count = count + weights[x]
    part_ref[0, cells:, :] = count[:, :chans].astype(BF)

    stacked = jnp.concatenate(weights, axis=0).astype(BF)
    flat = jnp.dot(stacked, spread[...], preferred_element_type=F32)
    ones = jnp.ones((cells, chans), BF)
    for x in range(rows):
        by_z = flat[x * zs : (x + 1) * zs] * same_z[...]
        by_y = jnp.sum(by_z, axis=0, keepdims=True) * same_y[...]
        select = jnp.concatenate([by_y, by_z], axis=0).astype(BF)
        sums = jnp.dot(select, feat_ref[x].reshape(cells, chans), preferred_element_type=F32)
        counts = jnp.dot(select, ones, preferred_element_type=F32)
        xy_ref[0, x] = (sums[:ys] * lax.rsqrt(1.0 + counts[:ys])).astype(BF)
        xz_acc[x] += sums[ys:]
        xz_cnt[x] += counts[ys:]

    for y in range(ys):
        total = None
        for x in range(rows):
            g = feat_ref[x, y].astype(F32) * jnp.broadcast_to(weights[x][:, y : y + 1], (zs, chans))
            total = g if total is None else total + g
        part_ref[0, y * zs : (y + 1) * zs, :] = total.astype(BF)

    @pl.when(step == pl.num_programs(0) - 1)
    def _():
        xz_ref[...] = (xz_acc[...] * lax.rsqrt(1.0 + xz_cnt[...])).astype(BF)


def pools(feat, occ, hgt, me, n):
    rows, y_len, zs, chans = feat.shape
    ys = y_len // n
    lanes = 128
    grid_spec = pltpu.PrefetchScalarGridSpec(
        num_scalar_prefetch=1,
        grid=(n,),
        in_specs=[
            pl.BlockSpec((rows, ys, zs, chans), lambda i, w: (0, i, 0, 0)),
            pl.BlockSpec((rows, zs, lanes), lambda i, w: (0, 0, i * ys // lanes)),
            pl.BlockSpec((rows, lanes), lambda i, w: (0, i * ys // lanes)),
        ],
        out_specs=[
            pl.BlockSpec((1, ys * zs + zs, chans), lambda i, w: (position(i ^ w[0], n), 0, 0)),
            pl.BlockSpec((1, rows, ys, chans), lambda i, w: (i, 0, 0, 0)),
            pl.BlockSpec((rows, zs, chans), lambda i, w: (0, 0, 0)),
        ],
        scratch_shapes=[
            pltpu.VMEM((rows, zs, chans), F32),
            pltpu.VMEM((rows, zs, chans), F32),
            pltpu.VMEM((lanes, ys * zs), BF),
            pltpu.VMEM((zs, ys * zs), F32),
            pltpu.VMEM((ys, ys * zs), F32),
        ],
    )
    hbm = lambda a: pltpu.with_memory_space_constraint(a, pltpu.MemorySpace.HBM)
    return pl.pallas_call(
        pool_body,
        grid_spec=grid_spec,
        out_shape=[
            jax.ShapeDtypeStruct((n, ys * zs + zs, chans), BF),
            jax.ShapeDtypeStruct((n, rows, ys, chans), BF),
            jax.ShapeDtypeStruct((rows, zs, chans), BF),
        ],
        compiler_params=pltpu.CompilerParams(vmem_limit_bytes=24 << 20),
        cost_estimate=pl.CostEstimate(flops=8 * feat.size, bytes_accessed=2 * feat.size, transcendentals=0),
        name="pools",
    )(me.reshape(1), hbm(feat), hbm(occ), hbm(hgt))


def planes_body(xy_ref, xz_ref, xy_in, xy_out, xz_in, xz_out, xy_plane, xz_plane):
    size = min(256, xy_ref.shape[0])
    for r in range(0, xy_ref.shape[0], size):
        xy_plane[r : r + size] = mlp(xy_ref[r : r + size], 0.5 * xy_in[...], xy_out[...])
    xz_plane[...] = mlp(xz_ref[...], 0.5 * xz_in[...], xz_out[...])


def planes(xy_pool, xz_pool, xy_in, xy_out, xz_in, xz_out):
    vmem = pl.BlockSpec(memory_space=pltpu.VMEM)
    flops = 4 * (xy_pool.size + xz_pool.size) * xy_in.shape[1]
    return pl.pallas_call(
        planes_body,
        in_specs=[vmem] * 6,
        out_specs=[vmem] * 2,
        out_shape=[jax.ShapeDtypeStruct(xy_pool.shape, BF), jax.ShapeDtypeStruct(xz_pool.shape, BF)],
        compiler_params=pltpu.CompilerParams(vmem_limit_bytes=16 << 20),
        cost_estimate=pl.CostEstimate(flops=flops, bytes_accessed=1 << 20, transcendentals=0),
        name="planes",
    )(xy_pool, xz_pool, xy_in, xy_out, xz_in, xz_out)


def yz_body(parts, zs, *refs):
    w_in, w_out, out = refs[parts:]
    total = refs[0][...].astype(F32)
    for ref in refs[1:parts]:
        total = total + ref[...].astype(F32)
    cells, chans = out.shape
    scale = lax.rsqrt(1.0 + total[cells:])
    pool = [
        total[r : r + zs] * jnp.broadcast_to(scale[:, y : y + 1], (zs, chans))
        for y, r in enumerate(range(0, cells, zs))
    ]
    out[...] = mlp(jnp.concatenate(pool, axis=0).astype(BF), 0.5 * w_in[...], w_out[...])


def yz_mlp(parts, zs, w_in, w_out):
    vmem = pl.BlockSpec(memory_space=pltpu.VMEM)
    cells, chans = parts[0].shape[0] - zs, parts[0].shape[1]
    return pl.pallas_call(
        functools.partial(yz_body, len(parts), zs),
        in_specs=[vmem] * (len(parts) + 2),
        out_specs=vmem,
        out_shape=jax.ShapeDtypeStruct((cells, chans), BF),
        compiler_params=pltpu.CompilerParams(vmem_limit_bytes=16 << 20),
        cost_estimate=pl.CostEstimate(flops=4 * cells * w_in.size, bytes_accessed=1 << 19, transcendentals=0),
        name="yz_mlp",
    )(*parts, w_in, w_out)


def voxel_body(which, feat_ref, xy_ref, xz_ref, yz_ref, w_in, w_out, out_ref):
    rows, ys, zs, chans = feat_ref.shape
    yz = yz_ref[0].astype(F32)
    half = 0.5 * w_in[...]
    for x in range(rows):
        xy = xy_ref[0, x].astype(F32)
        xz = xz_ref[x].astype(F32)
        mixed = feat_ref[x].astype(F32) + xy[:, None, :] + xz[None, :, :]
        mixed = (mixed.reshape(ys * zs, chans) + yz).astype(BF)
        out_ref[x] = mlp(mixed, half, w_out[...]).reshape(ys, zs, chans)


def voxels(feat, xy_plane, xz_plane, yz_plane, w_in, w_out, me, n):
    rows, y_len, zs, chans = feat.shape
    ys = y_len // n
    which = me.reshape(1)
    chunk = lambda i, w: offset(i, n) ^ w[0]
    whole = lambda a: pl.BlockSpec(a.shape, lambda i, w: (0,) * a.ndim)
    grid_spec = pltpu.PrefetchScalarGridSpec(
        num_scalar_prefetch=1,
        grid=(n,),
        in_specs=[
            pl.BlockSpec((rows, ys, zs, chans), lambda i, w: (0, chunk(i, w), 0, 0)),
            pl.BlockSpec((1, rows, ys, chans), lambda i, w: (chunk(i, w), 0, 0, 0)),
            whole(xz_plane),
            pl.BlockSpec((1, ys * zs, chans), lambda i, w: (i, 0, 0)),
            whole(w_in),
            whole(w_out),
        ],
        out_specs=pl.BlockSpec((rows, ys, zs, chans), lambda i, w: (0, chunk(i, w), 0, 0)),
    )
    return pl.pallas_call(
        voxel_body,
        grid_spec=grid_spec,
        out_shape=jax.ShapeDtypeStruct(feat.shape, BF),
        compiler_params=pltpu.CompilerParams(vmem_limit_bytes=24 << 20),
        cost_estimate=pl.CostEstimate(
            flops=4 * feat.size * w_in.shape[1], bytes_accessed=4 * feat.size, transcendentals=0
        ),
        name="voxels",
    )(which, feat, xy_plane, xz_plane, yz_plane, w_in, w_out)


def swap(value, n, offset):
    return lax.ppermute(value, "gx", [(i, i ^ offset) for i in range(n)])


def per_device(n, features, occupancy, heights, xy_in, xy_out, xz_in, xz_out, yz_in, yz_out, voxel_in, voxel_out):
    zs = features.shape[2]
    me = lax.axis_index("gx")
    parts, xy_pool, xz_pool = pools(features, jnp.swapaxes(occupancy, 1, 2), heights, me, n)
    chans = features.shape[3]
    xy_plane, xz_plane = planes(
        xy_pool.reshape(-1, chans), xz_pool.reshape(-1, chans), xy_in, xy_out, xz_in, xz_out
    )
    xy_plane, xz_plane = xy_plane.reshape(xy_pool.shape), xz_plane.reshape(xz_pool.shape)

    digits = radices(n)
    weights = [1]
    for digit in digits:
        weights.append(weights[-1] * digit)
    held = parts
    pieces = None
    for stage, digit in enumerate(digits):
        size = held.shape[0] // digit
        pieces = [held[:size]] + [
            swap(held[d * size : (d + 1) * size], n, d * weights[stage]) for d in range(1, digit)
        ]
        if stage == 1:
            pieces, xy_plane, xz_plane = lax.optimization_barrier((pieces, xy_plane, xz_plane))
        if stage < len(digits) - 1:
            held = sum(piece.astype(F32) for piece in pieces).astype(BF)
    plane = yz_mlp([piece[0] for piece in pieces], zs, yz_in, yz_out)[None]
    for stage, digit in reversed(list(enumerate(digits))):
        plane = jnp.concatenate([plane] + [swap(plane, n, d * weights[stage]) for d in range(1, digit)], axis=0)
    return voxels(features, xy_plane, xz_plane, plane, voxel_in, voxel_out, me, n)


def solution(mesh):
    split = ("group", "gx")
    in_specs = (P(split, None, None, None), P(split, None, None), P(split, None)) + (P(),) * 8
    return jax.shard_map(
        functools.partial(per_device, mesh.shape["gx"]),
        mesh=mesh,
        in_specs=in_specs,
        out_specs=P(split, None, None, None),
        check_vma=False,
    )
```

```python
import functools

import jax
import jax.numpy as jnp
from jax import lax
from jax.experimental import pallas as pl
from jax.experimental.pallas import tpu as pltpu
from jax.sharding import PartitionSpec as P


BF = jnp.bfloat16
F32 = jnp.float32


def radices(n):
    digits, left = [2], n // 2
    while left > 1:
        digits.append(4 if left % 4 == 0 else 2)
        left //= digits[-1]
    return digits


def offset(pos, n):
    off, slower, weight = 0, n, 1
    for digit in radices(n):
        slower //= digit
        off = off + ((pos // slower) % digit) * weight
        weight *= digit
    return off


def silu(half):
    return half + half * jnp.tanh(half)


def mlp(x, w_in, w_out):
    hidden = silu(jnp.dot(x, w_in, preferred_element_type=F32)).astype(BF)
    return jnp.dot(hidden, w_out, preferred_element_type=F32).astype(BF)


def position(off, n):
    pos, slower, weight = 0, n, 1
    for digit in radices(n):
        slower //= digit
        pos = pos + ((off // weight) % digit) * slower
        weight *= digit
    return pos


def pool_body(
    n, me_ref, feat_hbm, occ_hbm, hgt_hbm, part_ref, xy_ref, xz_ref,
    feat_ref, occ_ref, hgt_ref, by_z_ref, by_cell_ref, wide_ref, picks_ref, scale_ref, seen_ref, xz_acc, feat_sems,
    side_sems,
):
    rows, y_len, zs, chans = feat_ref.shape
    ys = y_len // n
    tiles, cells, _ = wide_ref.shape
    tile_y, lanes, stack = cells // zs, chans, rows * zs
    both = tile_y + zs

    def fetch(t):
        at = pl.ds(t * tile_y, tile_y)
        return pltpu.make_async_copy(feat_hbm.at[:, at], feat_ref.at[:, at], feat_sems.at[t])

    sides = [
        pltpu.make_async_copy(occ_hbm, occ_ref, side_sems.at[0]),
        pltpu.make_async_copy(hgt_hbm, hgt_ref, side_sems.at[1]),
    ]
    for side in sides:
        side.start()
    lax.fori_loop(0, tiles, lambda t, _: fetch(t).start(), None)

    iota = lambda shape, axis: lax.broadcasted_iota(jnp.int32, shape, axis)
    widen = (iota((stack, rows * chans), 0) // zs == iota((stack, rows * chans), 1) // chans).astype(F32).astype(BF)
    same_z = (iota((stack, cells), 0) % zs == iota((stack, cells), 1) % zs).astype(F32)
    same_y = (iota((tile_y, cells), 0) == iota((tile_y, cells), 1) // zs).astype(F32)
    zidx = iota((zs, lanes), 0)
    for side in sides:
        side.wait()

    parts = lanes // tile_y
    spread = (iota((lanes, parts * cells), 0) == iota((lanes, parts * cells), 1) // zs).astype(F32).astype(BF)
    xz_count = [0.0] * rows
    for block in range(y_len // lanes):
        at = slice(block * lanes, (block + 1) * lanes)
        weights = [
            jnp.where(zidx < hgt_ref[x : x + 1, at], occ_ref[x, :, at], 0).astype(F32) for x in range(rows)
        ]
        seen_ref[block] = sum(weights[1:], weights[0])
        xy_count = [jnp.sum(w, axis=0, keepdims=True) for w in weights]
        xy_count += [jnp.zeros((1, lanes), F32)] * (8 - rows % 8)
        scale_ref[at, : len(xy_count)] = lax.rsqrt(1.0 + jnp.concatenate(xy_count, axis=0)).T
        for x in range(rows):
            xz_count[x] = xz_count[x] + jnp.sum(weights[x], axis=1, keepdims=True)
        stacked = jnp.concatenate(weights, axis=0).astype(BF)
        for part in range(parts):
            columns = slice(part * cells, (part + 1) * cells)
            by_z_ref[block * parts + part] = (
                jnp.dot(stacked, spread[:, columns], preferred_element_type=F32) * same_z
            )
    for t in range(tiles):
        by_cell_ref[t] = by_z_ref[t].T.astype(BF)
    for t in range(tiles):
        wide_ref[t] = jnp.dot(by_cell_ref[t], widen, preferred_element_type=F32)
    for t in range(tiles):
        picks = []
        for x in range(rows):
            row_z = by_z_ref[t, x * zs : (x + 1) * zs]
            picks += [jnp.sum(row_z, axis=0, keepdims=True) * same_y, row_z]
        picks_ref[t] = jnp.concatenate(picks, axis=0).astype(BF)

    xz_acc[...] = jnp.zeros_like(xz_acc)
    group = min(ys, tile_y)

    def tile(t, _):
        first = t * tile_y
        fetch(t).wait()
        for g in range(tile_y // group):
            start = first + g * group
            home, inner = position((start // ys) ^ me_ref[0], n), start % ys
            for y in range(group):
                cell = (g * group + y) * zs
                total = None
                for x in range(rows):
                    weight = wide_ref[t, cell : cell + zs, x * chans : (x + 1) * chans]
                    term = feat_ref[x, start + y].astype(F32) * weight
                    total = term if total is None else total + term
                at = y * zs if group == ys else pl.multiple_of((inner + y) * zs, zs)
                part_ref[home, pl.ds(at, zs), :] = total.astype(BF)
            shift = lax.rem(lanes - lax.rem(start - inner, lanes), lanes)
            part_ref[home, ys * zs :, :] = pltpu.roll(seen_ref[start // lanes], shift, 1).astype(BF)
        for x in range(rows):
            pick = slice(x * both, (x + 1) * both)
            cells_x = feat_ref[x, pl.ds(first, tile_y)].reshape(cells, chans)
            sums = jnp.dot(picks_ref[t, pick], cells_x, preferred_element_type=F32)
            scale = scale_ref[pl.ds(pl.multiple_of(first, tile_y), tile_y), x : x + 1]
            pool = (sums[:tile_y] * jnp.broadcast_to(scale, (tile_y, chans))).astype(BF)
            for g in range(tile_y // group):
                start = first + g * group
                at = slice(None) if group == ys else pl.ds(pl.multiple_of(start % ys, group), group)
                xy_ref[start // ys, x, at] = pool[g * group : (g + 1) * group]
            xz_acc[x] += sums[tile_y:]

    lax.fori_loop(0, tiles, tile, None)
    for x in range(rows):
        scale = lax.rsqrt(1.0 + jnp.broadcast_to(xz_count[x], (zs, chans)))
        xz_ref[x] = (xz_acc[x] * scale).astype(BF)


def pools(feat, occ, hgt, me, n):
    rows, y_len, zs, chans = feat.shape
    ys = y_len // n
    tile_y = 256 // zs
    tiles, cells = y_len // tile_y, tile_y * zs
    vmem = pl.BlockSpec(memory_space=pltpu.VMEM)
    hbm = pl.BlockSpec(memory_space=pltpu.MemorySpace.HBM)
    return pl.pallas_call(
        functools.partial(pool_body, n),
        in_specs=[pl.BlockSpec(memory_space=pltpu.SMEM), hbm, hbm, hbm],
        out_specs=[vmem] * 3,
        out_shape=[
            jax.ShapeDtypeStruct((n, ys * zs + zs, chans), BF),
            jax.ShapeDtypeStruct((n, rows, ys, chans), BF),
            jax.ShapeDtypeStruct((rows, zs, chans), BF),
        ],
        scratch_shapes=[
            pltpu.VMEM(feat.shape, BF),
            pltpu.VMEM(occ.shape, jnp.int32),
            pltpu.VMEM(hgt.shape, jnp.int32),
            pltpu.VMEM((tiles, rows * zs, cells), F32),
            pltpu.VMEM((tiles, cells, rows * zs), BF),
            pltpu.VMEM((tiles, cells, rows * chans), F32),
            pltpu.VMEM((tiles, rows * (tile_y + zs), cells), BF),
            pltpu.VMEM((y_len, 16), F32),
            pltpu.VMEM((y_len // chans, zs, chans), F32),
            pltpu.VMEM((rows, zs, chans), F32),
            pltpu.SemaphoreType.DMA((tiles,)),
            pltpu.SemaphoreType.DMA((2,)),
        ],
        compiler_params=pltpu.CompilerParams(vmem_limit_bytes=36 << 20),
        cost_estimate=pl.CostEstimate(flops=8 * feat.size, bytes_accessed=2 * feat.size, transcendentals=0),
        name="pools",
    )(me.reshape(1), *(pltpu.with_memory_space_constraint(a, pltpu.MemorySpace.HBM) for a in (feat, occ, hgt)))


def planes_body(xy_ref, xz_ref, xy_in, xy_out, xz_in, xz_out, xy_plane, xz_plane):
    size = min(256, xy_ref.shape[0])
    for r in range(0, xy_ref.shape[0], size):
        xy_plane[r : r + size] = mlp(xy_ref[r : r + size], 0.5 * xy_in[...], xy_out[...])
    xz_plane[...] = mlp(xz_ref[...], 0.5 * xz_in[...], xz_out[...])


def planes(xy_pool, xz_pool, xy_in, xy_out, xz_in, xz_out):
    vmem = pl.BlockSpec(memory_space=pltpu.VMEM)
    flops = 4 * (xy_pool.size + xz_pool.size) * xy_in.shape[1]
    return pl.pallas_call(
        planes_body,
        in_specs=[vmem] * 6,
        out_specs=[vmem] * 2,
        out_shape=[jax.ShapeDtypeStruct(xy_pool.shape, BF), jax.ShapeDtypeStruct(xz_pool.shape, BF)],
        compiler_params=pltpu.CompilerParams(vmem_limit_bytes=16 << 20),
        cost_estimate=pl.CostEstimate(flops=flops, bytes_accessed=1 << 20, transcendentals=0),
        name="planes",
    )(xy_pool, xz_pool, xy_in, xy_out, xz_in, xz_out)


def yz_body(parts, zs, *refs):
    w_in, w_out, out = refs[parts:]
    total = refs[0][...].astype(F32)
    for ref in refs[1:parts]:
        total = total + ref[...].astype(F32)
    cells, chans = out.shape
    scale = lax.rsqrt(1.0 + total[cells:])
    pool = [
        total[r : r + zs] * jnp.broadcast_to(scale[:, y : y + 1], (zs, chans))
        for y, r in enumerate(range(0, cells, zs))
    ]
    out[...] = mlp(jnp.concatenate(pool, axis=0).astype(BF), 0.5 * w_in[...], w_out[...])


def yz_mlp(parts, zs, w_in, w_out):
    vmem = pl.BlockSpec(memory_space=pltpu.VMEM)
    cells, chans = parts[0].shape[0] - zs, parts[0].shape[1]
    return pl.pallas_call(
        functools.partial(yz_body, len(parts), zs),
        in_specs=[vmem] * (len(parts) + 2),
        out_specs=vmem,
        out_shape=jax.ShapeDtypeStruct((cells, chans), BF),
        compiler_params=pltpu.CompilerParams(vmem_limit_bytes=16 << 20),
        cost_estimate=pl.CostEstimate(flops=4 * cells * w_in.size, bytes_accessed=1 << 19, transcendentals=0),
        name="yz_mlp",
    )(*parts, w_in, w_out)


def voxel_body(which, feat_ref, xy_ref, xz_ref, yz_ref, w_in, w_out, out_ref):
    rows, ys, zs, chans = feat_ref.shape
    yz = yz_ref[0].astype(F32)
    half = 0.5 * w_in[...]
    for x in range(rows):
        xy = xy_ref[0, x].astype(F32)
        xz = xz_ref[x].astype(F32)
        mixed = feat_ref[x].astype(F32) + xy[:, None, :] + xz[None, :, :]
        mixed = (mixed.reshape(ys * zs, chans) + yz).astype(BF)
        out_ref[x] = mlp(mixed, half, w_out[...]).reshape(ys, zs, chans)


def voxels(feat, xy_plane, xz_plane, yz_plane, w_in, w_out, me, n):
    rows, y_len, zs, chans = feat.shape
    ys = y_len // n
    which = me.reshape(1)
    chunk = lambda i, w: offset(i, n) ^ w[0]
    whole = lambda a: pl.BlockSpec(a.shape, lambda i, w: (0,) * a.ndim)
    grid_spec = pltpu.PrefetchScalarGridSpec(
        num_scalar_prefetch=1,
        grid=(n,),
        in_specs=[
            pl.BlockSpec((rows, ys, zs, chans), lambda i, w: (0, chunk(i, w), 0, 0)),
            pl.BlockSpec((1, rows, ys, chans), lambda i, w: (chunk(i, w), 0, 0, 0)),
            whole(xz_plane),
            pl.BlockSpec((1, ys * zs, chans), lambda i, w: (i, 0, 0)),
            whole(w_in),
            whole(w_out),
        ],
        out_specs=pl.BlockSpec((rows, ys, zs, chans), lambda i, w: (0, chunk(i, w), 0, 0)),
    )
    return pl.pallas_call(
        voxel_body,
        grid_spec=grid_spec,
        out_shape=jax.ShapeDtypeStruct(feat.shape, BF),
        compiler_params=pltpu.CompilerParams(vmem_limit_bytes=24 << 20),
        cost_estimate=pl.CostEstimate(
            flops=4 * feat.size * w_in.shape[1], bytes_accessed=4 * feat.size, transcendentals=0
        ),
        name="voxels",
    )(which, feat, xy_plane, xz_plane, yz_plane, w_in, w_out)


def swap(value, n, offset):
    return lax.ppermute(value, "gx", [(i, i ^ offset) for i in range(n)])


def per_device(n, features, occupancy, heights, xy_in, xy_out, xz_in, xz_out, yz_in, yz_out, voxel_in, voxel_out):
    zs = features.shape[2]
    me = lax.axis_index("gx")
    parts, xy_pool, xz_pool = pools(features, jnp.swapaxes(occupancy, 1, 2), heights, me, n)
    chans = features.shape[3]
    xy_plane, xz_plane = planes(
        xy_pool.reshape(-1, chans), xz_pool.reshape(-1, chans), xy_in, xy_out, xz_in, xz_out
    )
    xy_plane, xz_plane = xy_plane.reshape(xy_pool.shape), xz_plane.reshape(xz_pool.shape)

    digits = radices(n)
    weights = [1]
    for digit in digits:
        weights.append(weights[-1] * digit)
    held = parts
    pieces = None
    for stage, digit in enumerate(digits):
        size = held.shape[0] // digit
        pieces = [held[:size]] + [
            swap(held[d * size : (d + 1) * size], n, d * weights[stage]) for d in range(1, digit)
        ]
        if stage == 1:
            pieces, xy_plane, xz_plane = lax.optimization_barrier((pieces, xy_plane, xz_plane))
        if stage < len(digits) - 1:
            held = sum(piece.astype(F32) for piece in pieces).astype(BF)
    plane = yz_mlp([piece[0] for piece in pieces], zs, yz_in, yz_out)[None]
    for stage, digit in reversed(list(enumerate(digits))):
        plane = jnp.concatenate([plane] + [swap(plane, n, d * weights[stage]) for d in range(1, digit)], axis=0)
    return voxels(features, xy_plane, xz_plane, plane, voxel_in, voxel_out, me, n)


def solution(mesh):
    split = ("group", "gx")
    in_specs = (P(split, None, None, None), P(split, None, None), P(split, None)) + (P(),) * 8
    return jax.shard_map(
        functools.partial(per_device, mesh.shape["gx"]),
        mesh=mesh,
        in_specs=in_specs,
        out_specs=P(split, None, None, None),
        check_vma=False,
    )
```

```python
import functools

import jax
import jax.numpy as jnp
from jax import lax
from jax.experimental import pallas as pl
from jax.experimental.pallas import tpu as pltpu
from jax.sharding import PartitionSpec as P


BF = jnp.bfloat16
F32 = jnp.float32


def radices(n):
    digits, left = [2], n // 2
    while left > 1:
        digits.append(4 if left % 4 == 0 else 2)
        left //= digits[-1]
    return digits


def mask(digit, weight):
    return digit * weight ^ (1 if weight == 2 else 0)


def offset(pos, n):
    off, slower, weight = 0, n, 1
    for digit in radices(n):
        slower //= digit
        value = (pos // slower) % digit
        crossed = jnp.minimum(value, 1) if weight == 2 else 0
        off = off ^ (value * weight) ^ crossed
        weight *= digit
    return off


def silu(half):
    return half + half * jnp.tanh(half)


def mlp(x, w_in, w_out):
    hidden = silu(jnp.dot(x, w_in, preferred_element_type=F32)).astype(BF)
    return jnp.dot(hidden, w_out, preferred_element_type=F32).astype(BF)


def position(off, n):
    pos, slower, weight, core = 0, n, 1, off % 2
    for digit in radices(n):
        slower //= digit
        if weight > 1:
            value = (off // weight) % digit
            pos = pos + value * slower
            core = core ^ jnp.minimum(value, 1) if weight == 2 else core
        weight *= digit
    return pos + core * (n // 2)


def pool_body(
    n, me_ref, feat_hbm, occ_hbm, hgt_hbm, part_ref, xy_ref, xz_ref, feat_ref,
    occ_ref, hgt_ref, by_z_ref, by_cell_ref, wide_ref, picks_ref, scale_ref, seen_ref, xz_acc, feat_sems,
    side_sems,
):
    rows, y_len, zs, chans = feat_ref.shape
    ys = y_len // n
    tiles, cells, _ = wide_ref.shape
    tile_y, lanes, stack = cells // zs, chans, rows * zs
    both = tile_y + zs

    def fetch(t):
        at = pl.ds(t * tile_y, tile_y)
        return pltpu.make_async_copy(feat_hbm.at[:, at], feat_ref.at[:, at], feat_sems.at[t])

    sides = [
        pltpu.make_async_copy(occ_hbm, occ_ref, side_sems.at[0]),
        pltpu.make_async_copy(hgt_hbm, hgt_ref, side_sems.at[1]),
    ]
    for side in sides:
        side.start()
    lax.fori_loop(0, tiles, lambda t, _: fetch(t).start(), None)

    iota = lambda shape, axis: lax.broadcasted_iota(jnp.int32, shape, axis)
    widen = (iota((stack, rows * chans), 0) // zs == iota((stack, rows * chans), 1) // chans).astype(F32).astype(BF)
    same_z = (iota((stack, cells), 0) % zs == iota((stack, cells), 1) % zs).astype(F32)
    same_y = (iota((tile_y, cells), 0) == iota((tile_y, cells), 1) // zs).astype(F32)
    zidx = iota((zs, lanes), 0)
    for side in sides:
        side.wait()

    parts = lanes // tile_y
    spread = (iota((lanes, parts * cells), 0) == iota((lanes, parts * cells), 1) // zs).astype(F32).astype(BF)
    xz_count = [0.0] * rows
    for block in range(y_len // lanes):
        at = slice(block * lanes, (block + 1) * lanes)
        weights = [
            jnp.where(zidx < hgt_ref[x : x + 1, at], occ_ref[x, :, at], 0).astype(F32) for x in range(rows)
        ]
        seen_ref[block] = sum(weights[1:], weights[0])
        xy_count = [jnp.sum(w, axis=0, keepdims=True) for w in weights]
        xy_count += [jnp.zeros((1, lanes), F32)] * (8 - rows % 8)
        scale_ref[at, : len(xy_count)] = lax.rsqrt(1.0 + jnp.concatenate(xy_count, axis=0)).T
        for x in range(rows):
            xz_count[x] = xz_count[x] + jnp.sum(weights[x], axis=1, keepdims=True)
        stacked = jnp.concatenate(weights, axis=0).astype(BF)
        for part in range(parts):
            columns = slice(part * cells, (part + 1) * cells)
            by_z_ref[block * parts + part] = (
                jnp.dot(stacked, spread[:, columns], preferred_element_type=F32) * same_z
            )
    for t in range(tiles):
        by_cell_ref[t] = by_z_ref[t].T.astype(BF)
    for t in range(tiles):
        wide_ref[t] = jnp.dot(by_cell_ref[t], widen, preferred_element_type=F32)
    for t in range(tiles):
        picks = []
        for x in range(rows):
            row_z = by_z_ref[t, x * zs : (x + 1) * zs]
            picks += [jnp.sum(row_z, axis=0, keepdims=True) * same_y, row_z]
        picks_ref[t] = jnp.concatenate(picks, axis=0).astype(BF)

    xz_acc[...] = jnp.zeros_like(xz_acc)
    group = min(ys, tile_y)

    def tile(t, _):
        first = t * tile_y
        fetch(t).wait()
        for g in range(tile_y // group):
            start = first + g * group
            home, inner = position((start // ys) ^ me_ref[0], n), start % ys
            for y in range(group):
                cell = (g * group + y) * zs
                total = None
                for x in range(rows):
                    weight = wide_ref[t, cell : cell + zs, x * chans : (x + 1) * chans]
                    term = feat_ref[x, start + y].astype(F32) * weight
                    total = term if total is None else total + term
                at = y * zs if group == ys else pl.multiple_of((inner + y) * zs, zs)
                part_ref[home, pl.ds(at, zs), :] = total.astype(BF)
            shift = lax.rem(lanes - lax.rem(start - inner, lanes), lanes)
            part_ref[home, ys * zs :, :] = pltpu.roll(seen_ref[start // lanes], shift, 1).astype(BF)
        for x in range(rows):
            pick = slice(x * both, (x + 1) * both)
            cells_x = feat_ref[x, pl.ds(first, tile_y)].reshape(cells, chans)
            sums = jnp.dot(picks_ref[t, pick], cells_x, preferred_element_type=F32)
            scale = scale_ref[pl.ds(pl.multiple_of(first, tile_y), tile_y), x : x + 1]
            pool = (sums[:tile_y] * jnp.broadcast_to(scale, (tile_y, chans))).astype(BF)
            for g in range(tile_y // group):
                start = first + g * group
                at = slice(None) if group == ys else pl.ds(pl.multiple_of(start % ys, group), group)
                xy_ref[start // ys, x, at] = pool[g * group : (g + 1) * group]
            xz_acc[x] += sums[tile_y:]

    lax.fori_loop(0, tiles, tile, None)
    for x in range(rows):
        scale = lax.rsqrt(1.0 + jnp.broadcast_to(xz_count[x], (zs, chans)))
        xz_ref[x] = (xz_acc[x] * scale).astype(BF)


def pools(feat, occ, hgt, me, n):
    rows, y_len, zs, chans = feat.shape
    ys = y_len // n
    tile_y = 256 // zs
    tiles, cells = y_len // tile_y, tile_y * zs
    vmem = pl.BlockSpec(memory_space=pltpu.VMEM)
    hbm = pl.BlockSpec(memory_space=pltpu.MemorySpace.HBM)
    return pl.pallas_call(
        functools.partial(pool_body, n),
        in_specs=[pl.BlockSpec(memory_space=pltpu.SMEM), hbm, hbm, hbm],
        out_specs=[vmem] * 4,
        out_shape=[
            jax.ShapeDtypeStruct((n, ys * zs + zs, chans), BF),
            jax.ShapeDtypeStruct((n, rows, ys, chans), BF),
            jax.ShapeDtypeStruct((rows, zs, chans), BF),
            jax.ShapeDtypeStruct(feat.shape, BF),
        ],
        scratch_shapes=[
            pltpu.VMEM(occ.shape, jnp.int32),
            pltpu.VMEM(hgt.shape, jnp.int32),
            pltpu.VMEM((tiles, rows * zs, cells), F32),
            pltpu.VMEM((tiles, cells, rows * zs), BF),
            pltpu.VMEM((tiles, cells, rows * chans), F32),
            pltpu.VMEM((tiles, rows * (tile_y + zs), cells), BF),
            pltpu.VMEM((y_len, 16), F32),
            pltpu.VMEM((y_len // chans, zs, chans), F32),
            pltpu.VMEM((rows, zs, chans), F32),
            pltpu.SemaphoreType.DMA((tiles,)),
            pltpu.SemaphoreType.DMA((2,)),
        ],
        compiler_params=pltpu.CompilerParams(vmem_limit_bytes=24 << 20),
        cost_estimate=pl.CostEstimate(flops=8 * feat.size, bytes_accessed=2 * feat.size, transcendentals=0),
        name="pools",
    )(me.reshape(1), *(pltpu.with_memory_space_constraint(a, pltpu.MemorySpace.HBM) for a in (feat, occ, hgt)))


def planes_body(xy_ref, xz_ref, xy_in, xy_out, xz_in, xz_out, xy_plane, xz_plane):
    size = min(256, xy_ref.shape[0])
    for r in range(0, xy_ref.shape[0], size):
        xy_plane[r : r + size] = mlp(xy_ref[r : r + size], 0.5 * xy_in[...], xy_out[...])
    xz_plane[...] = mlp(xz_ref[...], 0.5 * xz_in[...], xz_out[...])


def planes(xy_pool, xz_pool, xy_in, xy_out, xz_in, xz_out):
    vmem = pl.BlockSpec(memory_space=pltpu.VMEM)
    flops = 4 * (xy_pool.size + xz_pool.size) * xy_in.shape[1]
    return pl.pallas_call(
        planes_body,
        in_specs=[vmem] * 6,
        out_specs=[vmem] * 2,
        out_shape=[jax.ShapeDtypeStruct(xy_pool.shape, BF), jax.ShapeDtypeStruct(xz_pool.shape, BF)],
        compiler_params=pltpu.CompilerParams(vmem_limit_bytes=8 << 20),
        cost_estimate=pl.CostEstimate(flops=flops, bytes_accessed=1 << 20, transcendentals=0),
        name="planes",
    )(xy_pool, xz_pool, xy_in, xy_out, xz_in, xz_out)


def yz_body(parts, zs, *refs):
    w_in, w_out, out = refs[parts:]
    total = refs[0][...].astype(F32)
    for ref in refs[1:parts]:
        total = total + ref[...].astype(F32)
    cells, chans = out.shape
    scale = lax.rsqrt(1.0 + total[cells:])
    pool = [
        total[r : r + zs] * jnp.broadcast_to(scale[:, y : y + 1], (zs, chans))
        for y, r in enumerate(range(0, cells, zs))
    ]
    out[...] = mlp(jnp.concatenate(pool, axis=0).astype(BF), 0.5 * w_in[...], w_out[...])


def yz_mlp(parts, zs, w_in, w_out):
    vmem = pl.BlockSpec(memory_space=pltpu.VMEM)
    cells, chans = parts[0].shape[0] - zs, parts[0].shape[1]
    return pl.pallas_call(
        functools.partial(yz_body, len(parts), zs),
        in_specs=[vmem] * (len(parts) + 2),
        out_specs=vmem,
        out_shape=jax.ShapeDtypeStruct((cells, chans), BF),
        compiler_params=pltpu.CompilerParams(vmem_limit_bytes=8 << 20),
        cost_estimate=pl.CostEstimate(flops=4 * cells * w_in.size, bytes_accessed=1 << 19, transcendentals=0),
        name="yz_mlp",
    )(*parts, w_in, w_out)


def first_body(feat_ref, xy_ref, xz_ref, w_in, out_ref):
    n, rows, ys, chans = xy_ref.shape
    zs = xz_ref.shape[1]
    half = 0.5 * w_in[...]

    def chunk(c, _):
        for x in range(rows):
            xy = xy_ref[c, x].astype(F32)
            part = feat_ref[x, pl.ds(c * ys, ys)].astype(F32) + xy[:, None, :] + xz_ref[x].astype(F32)[None]
            part = part.reshape(ys * zs, chans).astype(BF)
            out_ref[c, x] = jnp.dot(part, half, preferred_element_type=F32)

    lax.fori_loop(0, n, chunk, None)


def first_layer(feat, xy_plane, xz_plane, w_in):
    n, rows, ys, _ = xy_plane.shape
    vmem = pl.BlockSpec(memory_space=pltpu.VMEM)
    return pl.pallas_call(
        first_body,
        in_specs=[vmem] * 4,
        out_specs=vmem,
        out_shape=jax.ShapeDtypeStruct((n, rows, ys * xz_plane.shape[1], w_in.shape[1]), F32),
        compiler_params=pltpu.CompilerParams(vmem_limit_bytes=8 << 20),
        cost_estimate=pl.CostEstimate(flops=2 * feat.size * w_in.shape[1], bytes_accessed=1 << 20, transcendentals=0),
        name="first_layer",
    )(feat, xy_plane, xz_plane, w_in)


def voxel_body(n, groups, before, last, me_ref, first_ref, w_in, w_out, *refs):
    yz_refs, refs = refs[: len(groups)], refs[len(groups) :]
    if before:
        prev_ref, refs = refs[0], refs[2:]
    out_hbm, done_ref, sems = refs
    _, rows, ys, zs, chans = done_ref.shape
    half = 0.5 * w_in[...]

    def send(source, index, pos, sem):
        at = pl.ds((offset(pos, n) ^ me_ref[0]) * ys, ys)
        return pltpu.make_async_copy(source.at[index], out_hbm.at[:, at], sems.at[sem])

    copies = [send(prev_ref, j, pos, j) for j, pos in enumerate(before)]
    for copy in copies:
        copy.start()
    slot = 0
    for yz_ref, (pos0, count) in zip(yz_refs, groups):

        def chunk(j, _, yz_ref=yz_ref, pos0=pos0, slot=slot):
            home = offset(pos0 + j, n) ^ me_ref[0]
            yz = jnp.dot(yz_ref[j], half, preferred_element_type=F32)
            for x in range(rows):
                hidden = silu(first_ref[home, x] + yz).astype(BF)
                cells = jnp.dot(hidden, w_out[...], preferred_element_type=F32).astype(BF)
                done_ref[slot + j, x] = cells.reshape(ys, zs, chans)
            if last:
                send(done_ref, slot + j, pos0 + j, len(before) + slot + j).start()

        lax.fori_loop(0, count, chunk, None)
        slot += count
    if last:
        slot = 0
        for pos0, count in groups:
            copies += [send(done_ref, slot + j, pos0 + j, len(before) + slot + j) for j in range(count)]
            slot += count
    for copy in copies:
        copy.wait()


def voxels(state, n, groups, yz, last, me, shape, first, w_in, w_out):
    rows, y_len, zs, chans = shape
    ys, size = y_len // n, sum(count for _, count in groups)
    before, extra = ([], []) if state is None else (state[0], list(state[1:]))
    vmem = pl.BlockSpec(memory_space=pltpu.VMEM)
    hbm = pl.BlockSpec(memory_space=pltpu.MemorySpace.HBM)
    done = (size, rows, ys, zs, chans)
    operands = [me.reshape(1), first, w_in, w_out, *yz, *extra]
    sems = pltpu.SemaphoreType.DMA((len(before) + (size if last else 0) or 1,))
    out = pl.pallas_call(
        functools.partial(voxel_body, n, groups, before, last),
        in_specs=[pl.BlockSpec(memory_space=pltpu.SMEM)] + [vmem] * (3 + len(yz)) + [vmem, hbm][: len(extra)],
        out_specs=[hbm] if last else [hbm, vmem],
        out_shape=[jax.ShapeDtypeStruct(shape, BF)] + ([] if last else [jax.ShapeDtypeStruct(done, BF)]),
        scratch_shapes=([pltpu.VMEM(done, BF)] if last else []) + [sems],
        input_output_aliases={len(operands) - 1: 0} if extra else {},
        compiler_params=pltpu.CompilerParams(vmem_limit_bytes=8 << 20, has_side_effects=True),
        cost_estimate=pl.CostEstimate(
            flops=4 * size * rows * ys * zs * w_in.size, bytes_accessed=1 << 20, transcendentals=0
        ),
        name="voxels",
    )(*operands)
    if last:
        return out[0]
    return [pos0 + j for pos0, count in groups for j in range(count)], out[1], out[0]


def swap(value, n, offset):
    return lax.ppermute(value, "gx", [(i, i ^ offset) for i in range(n)])


def per_device(n, features, occupancy, heights, xy_in, xy_out, xz_in, xz_out, yz_in, yz_out, voxel_in, voxel_out):
    zs = features.shape[2]
    me = lax.axis_index("gx")
    parts, xy_pool, xz_pool, feat = pools(features, jnp.swapaxes(occupancy, 1, 2), heights, me, n)
    chans = features.shape[3]
    xy_plane, xz_plane = planes(
        xy_pool.reshape(-1, chans), xz_pool.reshape(-1, chans), xy_in, xy_out, xz_in, xz_out
    )
    first = first_layer(feat, xy_plane.reshape(xy_pool.shape), xz_plane.reshape(xz_pool.shape), voxel_in)

    digits = radices(n)
    weights = [1]
    for digit in digits:
        weights.append(weights[-1] * digit)
    held = parts
    pieces = None
    for stage, digit in enumerate(digits):
        size = held.shape[0] // digit
        pieces = [held[:size]] + [
            swap(held[d * size : (d + 1) * size], n, mask(d, weights[stage])) for d in range(1, digit)
        ]
        if stage == 1:
            pieces, first = lax.optimization_barrier((pieces, first))
        if stage < len(digits) - 1:
            held = sum(piece.astype(F32) for piece in pieces).astype(BF)
    plane = yz_mlp([piece[0] for piece in pieces], zs, yz_in, yz_out)[None]
    call = functools.partial(
        voxels, me=me, shape=features.shape, first=first, w_in=voxel_in, w_out=voxel_out
    )
    sibling, slower, waiting = n // 2, 1, []
    state = call(None, n, [(0, 1)], [plane], False)
    own = state[0]
    for stage, digit in reversed(list(enumerate(digits))[1:]):
        arrived = []
        for d in range(1, digit):
            arrived.append(swap(plane, n, mask(d, weights[stage])))
        if slower == 1:
            arrived, state = lax.optimization_barrier((arrived, state[1:]))
            plane = jnp.concatenate([plane] + arrived, axis=0)
            groups = [(d, 1) for d in range(1, digit)] + [(sibling, digit)]
            passed = swap(plane, n, 1)
            state = call((own, *state), n, groups, arrived + [passed], False)
        else:
            for d, piece in enumerate(arrived, 1):
                piece, *tail = lax.optimization_barrier((piece, *state[1:]))
                state = (state[0], *tail)
                pieces = waiting + [((d * slower, slower), piece)]
                waiting = [((sibling + d * slower, slower), swap(piece, n, 1))]
                state = call(state, n, [g for g, _ in pieces], [p for _, p in pieces], False)
            plane = jnp.concatenate([plane] + arrived, axis=0)
        slower *= digit
    return call(state, n, [g for g, _ in waiting], [p for _, p in waiting], True)


def solution(mesh):
    split = ("group", "gx")
    in_specs = (P(split, None, None, None), P(split, None, None), P(split, None)) + (P(),) * 8
    n = mesh.shape["gx"]

    def body(*args):
        return per_device(n, *args)

    step = jax.shard_map(
        body, mesh=mesh, in_specs=in_specs, out_specs=P(split, None, None, None), check_vma=False
    )
    if len(radices(n)) > 3:
        return step
    return step
```

```python
import functools

import jax
import jax.numpy as jnp
from jax import lax
from jax.experimental import pallas as pl
from jax.experimental.pallas import tpu as pltpu
from jax.sharding import PartitionSpec as P


BF = jnp.bfloat16
F32 = jnp.float32


def radices(n):
    digits, left = [2], n // 2
    while left > 1:
        digits.append(4 if left % 4 == 0 else 2)
        left //= digits[-1]
    return digits


def mask(digit, weight):
    return digit * weight ^ (1 if weight == 2 else 0)


def offset(pos, n):
    off, slower, weight = 0, n, 1
    for digit in radices(n):
        slower //= digit
        value = (pos // slower) % digit
        crossed = jnp.minimum(value, 1) if weight == 2 else 0
        off = off ^ (value * weight) ^ crossed
        weight *= digit
    return off


def silu(half):
    return half + half * jnp.tanh(half)


def mlp(x, w_in, w_out):
    hidden = silu(jnp.dot(x, w_in, preferred_element_type=F32)).astype(BF)
    return jnp.dot(hidden, w_out, preferred_element_type=F32).astype(BF)


def position(off, n):
    pos, slower, weight, core = 0, n, 1, off % 2
    for digit in radices(n):
        slower //= digit
        if weight > 1:
            value = (off // weight) % digit
            pos = pos + value * slower
            core = core ^ jnp.minimum(value, 1) if weight == 2 else core
        weight *= digit
    return pos + core * (n // 2)


def pool_body(
    n, me_ref, feat_hbm, occ_hbm, hgt_hbm, part_ref, xy_ref, xz_ref, feat_ref,
    occ_ref, hgt_ref, by_z_ref, by_cell_ref, wide_ref, picks_ref, scale_ref, seen_ref, xz_acc, feat_sems,
    side_sems,
):
    rows, y_len, zs, chans = feat_ref.shape
    ys = y_len // n
    tiles, cells, _ = wide_ref.shape
    tile_y, lanes, stack = cells // zs, chans, rows * zs
    both = tile_y + zs

    def fetch(t):
        at = pl.ds(t * tile_y, tile_y)
        return pltpu.make_async_copy(feat_hbm.at[:, at], feat_ref.at[:, at], feat_sems.at[t])

    sides = [
        pltpu.make_async_copy(occ_hbm, occ_ref, side_sems.at[0]),
        pltpu.make_async_copy(hgt_hbm, hgt_ref, side_sems.at[1]),
    ]
    for side in sides:
        side.start()
    lax.fori_loop(0, tiles, lambda t, _: fetch(t).start(), None)

    iota = lambda shape, axis: lax.broadcasted_iota(jnp.int32, shape, axis)
    widen = (iota((stack, rows * chans), 0) // zs == iota((stack, rows * chans), 1) // chans).astype(F32).astype(BF)
    same_z = (iota((stack, cells), 0) % zs == iota((stack, cells), 1) % zs).astype(F32)
    same_y = (iota((tile_y, cells), 0) == iota((tile_y, cells), 1) // zs).astype(F32)
    zidx = iota((zs, lanes), 0)
    for side in sides:
        side.wait()

    parts = lanes // tile_y
    spread = (iota((lanes, parts * cells), 0) == iota((lanes, parts * cells), 1) // zs).astype(F32).astype(BF)
    xz_count = [0.0] * rows
    for block in range(y_len // lanes):
        at = slice(block * lanes, (block + 1) * lanes)
        weights = [
            jnp.where(zidx < hgt_ref[x : x + 1, at], occ_ref[x, :, at], 0).astype(F32) for x in range(rows)
        ]
        seen_ref[block] = sum(weights[1:], weights[0])
        xy_count = [jnp.sum(w, axis=0, keepdims=True) for w in weights]
        xy_count += [jnp.zeros((1, lanes), F32)] * (8 - rows % 8)
        scale_ref[at, : len(xy_count)] = lax.rsqrt(1.0 + jnp.concatenate(xy_count, axis=0)).T
        for x in range(rows):
            xz_count[x] = xz_count[x] + jnp.sum(weights[x], axis=1, keepdims=True)
        stacked = jnp.concatenate(weights, axis=0).astype(BF)
        for part in range(parts):
            columns = slice(part * cells, (part + 1) * cells)
            by_z_ref[block * parts + part] = (
                jnp.dot(stacked, spread[:, columns], preferred_element_type=F32) * same_z
            )
    for t in range(tiles):
        by_cell_ref[t] = by_z_ref[t].T.astype(BF)
    for t in range(tiles):
        wide_ref[t] = jnp.dot(by_cell_ref[t], widen, preferred_element_type=F32)
    for t in range(tiles):
        picks = []
        for x in range(rows):
            row_z = by_z_ref[t, x * zs : (x + 1) * zs]
            picks += [jnp.sum(row_z, axis=0, keepdims=True) * same_y, row_z]
        picks_ref[t] = jnp.concatenate(picks, axis=0).astype(BF)

    xz_acc[...] = jnp.zeros_like(xz_acc)
    group = min(ys, tile_y)

    def tile(t, _):
        first = t * tile_y
        fetch(t).wait()
        for g in range(tile_y // group):
            start = first + g * group
            home, inner = position((start // ys) ^ me_ref[0], n), start % ys
            for y in range(group):
                cell = (g * group + y) * zs
                total = None
                for x in range(rows):
                    weight = wide_ref[t, cell : cell + zs, x * chans : (x + 1) * chans]
                    term = feat_ref[x, start + y].astype(F32) * weight
                    total = term if total is None else total + term
                at = y * zs if group == ys else pl.multiple_of((inner + y) * zs, zs)
                part_ref[home, pl.ds(at, zs), :] = total.astype(BF)
            shift = lax.rem(lanes - lax.rem(start - inner, lanes), lanes)
            part_ref[home, ys * zs :, :] = pltpu.roll(seen_ref[start // lanes], shift, 1).astype(BF)
        for x in range(rows):
            pick = slice(x * both, (x + 1) * both)
            cells_x = feat_ref[x, pl.ds(first, tile_y)].reshape(cells, chans)
            sums = jnp.dot(picks_ref[t, pick], cells_x, preferred_element_type=F32)
            scale = scale_ref[pl.ds(pl.multiple_of(first, tile_y), tile_y), x : x + 1]
            pool = (sums[:tile_y] * jnp.broadcast_to(scale, (tile_y, chans))).astype(BF)
            for g in range(tile_y // group):
                start = first + g * group
                at = slice(None) if group == ys else pl.ds(pl.multiple_of(start % ys, group), group)
                xy_ref[start // ys, x, at] = pool[g * group : (g + 1) * group]
            xz_acc[x] += sums[tile_y:]

    lax.fori_loop(0, tiles, tile, None)
    for x in range(rows):
        scale = lax.rsqrt(1.0 + jnp.broadcast_to(xz_count[x], (zs, chans)))
        xz_ref[x] = (xz_acc[x] * scale).astype(BF)


def pools(feat, occ, hgt, me, n):
    rows, y_len, zs, chans = feat.shape
    ys = y_len // n
    tile_y = 256 // zs
    tiles, cells = y_len // tile_y, tile_y * zs
    vmem = pl.BlockSpec(memory_space=pltpu.VMEM)
    hbm = pl.BlockSpec(memory_space=pltpu.MemorySpace.HBM)
    return pl.pallas_call(
        functools.partial(pool_body, n),
        in_specs=[pl.BlockSpec(memory_space=pltpu.SMEM), hbm, hbm, hbm],
        out_specs=[vmem] * 4,
        out_shape=[
            jax.ShapeDtypeStruct((n, ys * zs + zs, chans), BF),
            jax.ShapeDtypeStruct((n, rows, ys, chans), BF),
            jax.ShapeDtypeStruct((rows, zs, chans), BF),
            jax.ShapeDtypeStruct(feat.shape, BF),
        ],
        scratch_shapes=[
            pltpu.VMEM(occ.shape, jnp.int32),
            pltpu.VMEM(hgt.shape, jnp.int32),
            pltpu.VMEM((tiles, rows * zs, cells), F32),
            pltpu.VMEM((tiles, cells, rows * zs), BF),
            pltpu.VMEM((tiles, cells, rows * chans), F32),
            pltpu.VMEM((tiles, rows * (tile_y + zs), cells), BF),
            pltpu.VMEM((y_len, 16), F32),
            pltpu.VMEM((y_len // chans, zs, chans), F32),
            pltpu.VMEM((rows, zs, chans), F32),
            pltpu.SemaphoreType.DMA((tiles,)),
            pltpu.SemaphoreType.DMA((2,)),
        ],
        compiler_params=pltpu.CompilerParams(vmem_limit_bytes=24 << 20),
        cost_estimate=pl.CostEstimate(flops=8 * feat.size, bytes_accessed=2 * feat.size, transcendentals=0),
        name="pools",
    )(me.reshape(1), *(pltpu.with_memory_space_constraint(a, pltpu.MemorySpace.HBM) for a in (feat, occ, hgt)))


def planes_body(xy_ref, xz_ref, xy_in, xy_out, xz_in, xz_out, xy_plane, xz_plane):
    size = min(256, xy_ref.shape[0])
    for r in range(0, xy_ref.shape[0], size):
        xy_plane[r : r + size] = mlp(xy_ref[r : r + size], 0.5 * xy_in[...], xy_out[...])
    xz_plane[...] = mlp(xz_ref[...], 0.5 * xz_in[...], xz_out[...])


def planes(xy_pool, xz_pool, xy_in, xy_out, xz_in, xz_out):
    vmem = pl.BlockSpec(memory_space=pltpu.VMEM)
    flops = 4 * (xy_pool.size + xz_pool.size) * xy_in.shape[1]
    return pl.pallas_call(
        planes_body,
        in_specs=[vmem] * 6,
        out_specs=[vmem] * 2,
        out_shape=[jax.ShapeDtypeStruct(xy_pool.shape, BF), jax.ShapeDtypeStruct(xz_pool.shape, BF)],
        compiler_params=pltpu.CompilerParams(vmem_limit_bytes=8 << 20),
        cost_estimate=pl.CostEstimate(flops=flops, bytes_accessed=1 << 20, transcendentals=0),
        name="planes",
    )(xy_pool, xz_pool, xy_in, xy_out, xz_in, xz_out)


def yz_body(parts, zs, *refs):
    w_in, w_out, out = refs[parts:]
    count, cells, chans = out.shape
    pools = []
    for u in range(count):
        total = refs[0][u].astype(F32)
        for v in range(1, parts):
            total = total + refs[v][u ^ v].astype(F32)
        scale = lax.rsqrt(1.0 + total[cells:])
        pools += [
            total[r : r + zs] * jnp.broadcast_to(scale[:, y : y + 1], (zs, chans))
            for y, r in enumerate(range(0, cells, zs))
        ]
    pool = jnp.concatenate(pools, axis=0).astype(BF)
    out[...] = mlp(pool, 0.5 * w_in[...], w_out[...]).reshape(count, cells, chans)


def yz_mlp(parts, zs, w_in, w_out):
    vmem = pl.BlockSpec(memory_space=pltpu.VMEM)
    count, rows, chans = parts[0].shape
    cells = rows - zs
    return pl.pallas_call(
        functools.partial(yz_body, len(parts), zs),
        in_specs=[vmem] * (len(parts) + 2),
        out_specs=vmem,
        out_shape=jax.ShapeDtypeStruct((count, cells, chans), BF),
        compiler_params=pltpu.CompilerParams(vmem_limit_bytes=8 << 20),
        cost_estimate=pl.CostEstimate(
            flops=4 * count * cells * w_in.size, bytes_accessed=1 << 19, transcendentals=0
        ),
        name="yz_mlp",
    )(*parts, w_in, w_out)


def first_body(feat_ref, xy_ref, xz_ref, w_in, out_ref):
    n, rows, ys, chans = xy_ref.shape
    zs = xz_ref.shape[1]
    half = 0.5 * w_in[...]

    def chunk(c, _):
        for x in range(rows):
            xy = xy_ref[c, x].astype(F32)
            part = feat_ref[x, pl.ds(c * ys, ys)].astype(F32) + xy[:, None, :] + xz_ref[x].astype(F32)[None]
            part = part.reshape(ys * zs, chans).astype(BF)
            out_ref[c, x] = jnp.dot(part, half, preferred_element_type=F32)

    lax.fori_loop(0, n, chunk, None)


def first_layer(feat, xy_plane, xz_plane, w_in):
    n, rows, ys, _ = xy_plane.shape
    vmem = pl.BlockSpec(memory_space=pltpu.VMEM)
    return pl.pallas_call(
        first_body,
        in_specs=[vmem] * 4,
        out_specs=vmem,
        out_shape=jax.ShapeDtypeStruct((n, rows, ys * xz_plane.shape[1], w_in.shape[1]), F32),
        compiler_params=pltpu.CompilerParams(vmem_limit_bytes=8 << 20),
        cost_estimate=pl.CostEstimate(flops=2 * feat.size * w_in.shape[1], bytes_accessed=1 << 20, transcendentals=0),
        name="first_layer",
    )(feat, xy_plane, xz_plane, w_in)


def voxel_body(n, groups, before, last, me_ref, first_ref, w_in, w_out, *refs):
    yz_refs, refs = refs[: len(groups)], refs[len(groups) :]
    if before:
        prev_ref, refs = refs[0], refs[2:]
    out_hbm, done_ref, own_ref, sems = refs
    _, rows, ys, zs, chans = done_ref.shape
    half = 0.5 * w_in[...]

    def send(source, index, pos, sem):
        at = pl.ds((offset(pos, n) ^ me_ref[0]) * ys, ys)
        return pltpu.make_async_copy(source.at[index], out_hbm.at[:, at], sems.at[sem])

    copies = [send(prev_ref, j, pos, j) for j, pos in enumerate(before)]
    for copy in copies:
        copy.start()
    slot = 0
    for yz_ref, (_, count) in zip(yz_refs, groups):
        both = yz_ref[...].reshape(count * ys * zs, chans)
        both = jnp.dot(both, half, preferred_element_type=F32)
        own_ref[slot : slot + count] = both.reshape(count, ys * zs, half.shape[1])
        slot += count
    slot = 0
    for yz_ref, (pos0, count) in zip(yz_refs, groups):

        def chunk(j, _, yz_ref=yz_ref, pos0=pos0, slot=slot):
            home = offset(pos0 + j, n) ^ me_ref[0]
            for x in range(0, rows, 3):
                hidden = silu(first_ref[home, x : x + 3] + own_ref[slot + j][None]).astype(BF)
                cells = jnp.dot(hidden.reshape(3 * ys * zs, -1), w_out[...], preferred_element_type=F32).astype(BF)
                done_ref[slot + j, x : x + 3] = cells.reshape(3, ys, zs, chans)
            if last:
                send(done_ref, slot + j, pos0 + j, len(before) + slot + j).start()

        lax.fori_loop(0, count, chunk, None)
        slot += count
    if last:
        slot = 0
        for pos0, count in groups:
            copies += [send(done_ref, slot + j, pos0 + j, len(before) + slot + j) for j in range(count)]
            slot += count
    for copy in copies:
        copy.wait()


def voxels(state, n, groups, yz, last, me, shape, first, w_in, w_out):
    rows, y_len, zs, chans = shape
    ys, size = y_len // n, sum(count for _, count in groups)
    before, extra = ([], []) if state is None else (state[0], list(state[1:]))
    vmem = pl.BlockSpec(memory_space=pltpu.VMEM)
    hbm = pl.BlockSpec(memory_space=pltpu.MemorySpace.HBM)
    done = (size, rows, ys, zs, chans)
    operands = [me.reshape(1), first, w_in, w_out, *yz, *extra]
    sems = pltpu.SemaphoreType.DMA((len(before) + (size if last else 0) or 1,))
    out = pl.pallas_call(
        functools.partial(voxel_body, n, groups, before, last),
        in_specs=[pl.BlockSpec(memory_space=pltpu.SMEM)] + [vmem] * (3 + len(yz)) + [vmem, hbm][: len(extra)],
        out_specs=[hbm] if last else [hbm, vmem],
        out_shape=[jax.ShapeDtypeStruct(shape, BF)] + ([] if last else [jax.ShapeDtypeStruct(done, BF)]),
        scratch_shapes=([pltpu.VMEM(done, BF)] if last else [])
        + [pltpu.VMEM((size, ys * zs, w_in.shape[1]), F32), sems],
        input_output_aliases={len(operands) - 1: 0} if extra else {},
        compiler_params=pltpu.CompilerParams(vmem_limit_bytes=20 << 20, has_side_effects=True),
        cost_estimate=pl.CostEstimate(
            flops=4 * size * rows * ys * zs * w_in.size, bytes_accessed=1 << 20, transcendentals=0
        ),
        name="voxels",
    )(*operands)
    if last:
        return out[0]
    return [pos0 + j for pos0, count in groups for j in range(count)], out[1], out[0]


def swap(value, n, offset):
    return lax.ppermute(value, "gx", [(i, i ^ offset) for i in range(n)])


def per_device(n, features, occupancy, heights, xy_in, xy_out, xz_in, xz_out, yz_in, yz_out, voxel_in, voxel_out):
    zs = features.shape[2]
    me = lax.axis_index("gx")
    parts, xy_pool, xz_pool, feat = pools(features, jnp.swapaxes(occupancy, 1, 2), heights, me, n)
    chans = features.shape[3]
    xy_plane, xz_plane = planes(
        xy_pool.reshape(-1, chans), xz_pool.reshape(-1, chans), xy_in, xy_out, xz_in, xz_out
    )
    first = first_layer(feat, xy_plane.reshape(xy_pool.shape), xz_plane.reshape(xz_pool.shape), voxel_in)

    digits = radices(n)
    weights = [1]
    for digit in digits:
        weights.append(weights[-1] * digit)
    held = parts
    for stage, digit in enumerate(digits[:-1]):
        size = held.shape[0] // digit
        pieces = [held[:size]] + [
            swap(held[d * size : (d + 1) * size], n, mask(d, weights[stage])) for d in range(1, digit)
        ]
        if stage == 1:
            pieces, first = lax.optimization_barrier((pieces, first))
        held = sum(piece.astype(F32) for piece in pieces).astype(BF)
    slower = digits[-1]
    pieces = [held] + [swap(held, n, mask(d, weights[len(digits) - 1])) for d in range(1, slower)]
    plane = yz_mlp(pieces, zs, yz_in, yz_out)

    call = functools.partial(voxels, me=me, shape=features.shape, first=first, w_in=voxel_in, w_out=voxel_out)
    sibling = n // 2
    passed = swap(plane, n, 1)
    state = call(None, n, [(0, slower)], [plane], False)
    state = call(state, n, [(sibling, slower)], [passed], False)
    waiting = []
    for stage, digit in reversed(list(enumerate(digits))[1:-1]):
        arrived = []
        for d in range(1, digit):
            arrived.append(swap(plane, n, mask(d, weights[stage])))
        for d, piece in enumerate(arrived, 1):
            piece, *tail = lax.optimization_barrier((piece, *state[1:]))
            state = (state[0], *tail)
            pieces = waiting + [((d * slower, slower), piece)]
            waiting = [((sibling + d * slower, slower), swap(piece, n, 1))]
            state = call(state, n, [g for g, _ in pieces], [p for _, p in pieces], False)
        plane = jnp.concatenate([plane] + arrived, axis=0)
        slower *= digit
    return call(state, n, [g for g, _ in waiting], [p for _, p in waiting], True)


def solution(mesh):
    split = ("group", "gx")
    in_specs = (P(split, None, None, None), P(split, None, None), P(split, None)) + (P(),) * 8
    n = mesh.shape["gx"]

    def body(*args):
        return per_device(n, *args)

    step = jax.shard_map(
        body, mesh=mesh, in_specs=in_specs, out_specs=P(split, None, None, None), check_vma=False
    )
    if len(radices(n)) > 3:
        return step
    return step
```

```python
import functools

import jax
import jax.numpy as jnp
from jax import lax
from jax.experimental import pallas as pl
from jax.experimental.pallas import tpu as pltpu
from jax.sharding import PartitionSpec as P


BF = jnp.bfloat16
F32 = jnp.float32


def radices(n):
    digits, left = [2], n // 2
    while left > 1:
        digits.append(4 if left % 4 == 0 else 2)
        left //= digits[-1]
    return digits


def mask(digit, weight):
    return digit * weight ^ (1 if weight == 2 else 0)


def offset(pos, n):
    off, slower, weight = 0, n, 1
    for digit in radices(n):
        slower //= digit
        value = (pos // slower) % digit
        crossed = jnp.minimum(value, 1) if weight == 2 else 0
        off = off ^ (value * weight) ^ crossed
        weight *= digit
    return off


def silu(half):
    return half + half * jnp.tanh(half)


def mlp(x, w_in, w_out):
    hidden = silu(jnp.dot(x, w_in, preferred_element_type=F32)).astype(BF)
    return jnp.dot(hidden, w_out, preferred_element_type=F32).astype(BF)


def position(off, n):
    pos, slower, weight, core = 0, n, 1, off % 2
    for digit in radices(n):
        slower //= digit
        if weight > 1:
            value = (off // weight) % digit
            pos = pos + value * slower
            core = core ^ jnp.minimum(value, 1) if weight == 2 else core
        weight *= digit
    return pos + core * (n // 2)


def partial_body(
    n, me_ref, feat_hbm, occ_hbm, hgt_hbm, part_ref, by_z_ref, feat_ref,
    occ_ref, hgt_ref, by_cell_ref, wide_ref, seen_ref, feat_sems, side_sems,
):
    rows, y_len, zs, chans = feat_ref.shape
    ys = y_len // n
    tiles, cells, _ = wide_ref.shape
    tile_y, lanes, stack = cells // zs, chans, rows * zs

    def fetch(t):
        at = pl.ds(t * tile_y, tile_y)
        return pltpu.make_async_copy(feat_hbm.at[:, at], feat_ref.at[:, at], feat_sems.at[t])

    sides = [
        pltpu.make_async_copy(occ_hbm, occ_ref, side_sems.at[0]),
        pltpu.make_async_copy(hgt_hbm, hgt_ref, side_sems.at[1]),
    ]
    for side in sides:
        side.start()
    lax.fori_loop(0, tiles, lambda t, _: fetch(t).start(), None)

    iota = lambda shape, axis: lax.broadcasted_iota(jnp.int32, shape, axis)
    widen = (iota((stack, rows * chans), 0) // zs == iota((stack, rows * chans), 1) // chans).astype(F32).astype(BF)
    same_z = (iota((stack, cells), 0) % zs == iota((stack, cells), 1) % zs).astype(F32)
    zidx = iota((zs, lanes), 0)
    parts = lanes // tile_y
    spread = (iota((lanes, parts * cells), 0) == iota((lanes, parts * cells), 1) // zs).astype(F32).astype(BF)
    for side in sides:
        side.wait()

    for block in range(y_len // lanes):
        at = slice(block * lanes, (block + 1) * lanes)
        weights = [
            jnp.where(zidx < hgt_ref[x : x + 1, at], occ_ref[x, :, at], 0).astype(F32) for x in range(rows)
        ]
        seen_ref[block] = sum(weights[1:], weights[0])
        stacked = jnp.concatenate(weights, axis=0).astype(BF)
        for part in range(parts):
            columns = slice(part * cells, (part + 1) * cells)
            by_z_ref[block * parts + part] = (
                jnp.dot(stacked, spread[:, columns], preferred_element_type=F32) * same_z
            )
    for t in range(tiles):
        by_cell_ref[t] = by_z_ref[t].T.astype(BF)
    for t in range(tiles):
        wide_ref[t] = jnp.dot(by_cell_ref[t], widen, preferred_element_type=F32)

    group = min(ys, tile_y)

    def tile(t, _):
        first = t * tile_y
        fetch(t).wait()
        for g in range(tile_y // group):
            start = first + g * group
            home, inner = position((start // ys) ^ me_ref[0], n), start % ys
            for y in range(group):
                cell = (g * group + y) * zs
                total = None
                for x in range(rows):
                    weight = wide_ref[t, cell : cell + zs, x * chans : (x + 1) * chans]
                    term = feat_ref[x, start + y].astype(F32) * weight
                    total = term if total is None else total + term
                at = y * zs if group == ys else pl.multiple_of((inner + y) * zs, zs)
                part_ref[home, pl.ds(at, zs), :] = total.astype(BF)
            shift = lax.rem(lanes - lax.rem(start - inner, lanes), lanes)
            part_ref[home, ys * zs :, :] = pltpu.roll(seen_ref[start // lanes], shift, 1).astype(BF)

    lax.fori_loop(0, tiles, tile, None)


def partials(feat, occ, hgt, me, n):
    rows, y_len, zs, chans = feat.shape
    ys = y_len // n
    tile_y = 256 // zs
    tiles, cells = y_len // tile_y, tile_y * zs
    vmem = pl.BlockSpec(memory_space=pltpu.VMEM)
    hbm = pl.BlockSpec(memory_space=pltpu.MemorySpace.HBM)
    return pl.pallas_call(
        functools.partial(partial_body, n),
        in_specs=[pl.BlockSpec(memory_space=pltpu.SMEM), hbm, hbm, hbm],
        out_specs=[vmem] * 3,
        out_shape=[
            jax.ShapeDtypeStruct((n, ys * zs + zs, chans), BF),
            jax.ShapeDtypeStruct((tiles, rows * zs, cells), F32),
            jax.ShapeDtypeStruct(feat.shape, BF),
        ],
        scratch_shapes=[
            pltpu.VMEM(occ.shape, jnp.int32),
            pltpu.VMEM(hgt.shape, jnp.int32),
            pltpu.VMEM((tiles, cells, rows * zs), BF),
            pltpu.VMEM((tiles, cells, rows * chans), F32),
            pltpu.VMEM((y_len // chans, zs, chans), F32),
            pltpu.SemaphoreType.DMA((tiles,)),
            pltpu.SemaphoreType.DMA((2,)),
        ],
        compiler_params=pltpu.CompilerParams(vmem_limit_bytes=24 << 20),
        cost_estimate=pl.CostEstimate(flops=8 * feat.size, bytes_accessed=2 * feat.size, transcendentals=0),
        name="partials",
    )(me.reshape(1), *(pltpu.with_memory_space_constraint(a, pltpu.MemorySpace.HBM) for a in (feat, occ, hgt)))


def pool_body(feat_ref, by_z_ref, xy_ref, xz_ref, xz_acc, xz_cnt):
    rows, _, zs, chans = feat_ref.shape
    _, _, ys, _ = xy_ref.shape
    tiles, _, cells = by_z_ref.shape
    tile_y = cells // zs
    both, group = tile_y + zs, min(ys, tile_y)
    iota = lambda axis: lax.broadcasted_iota(jnp.int32, (tile_y, cells), axis)
    same_y = (iota(0) == iota(1) // zs).astype(F32)
    ones = jnp.ones((cells, chans), BF)
    xz_acc[...] = jnp.zeros_like(xz_acc)
    xz_cnt[...] = jnp.zeros_like(xz_cnt)

    def tile(t, _):
        first = t * tile_y
        picks = []
        for x in range(rows):
            row_z = by_z_ref[t, x * zs : (x + 1) * zs]
            picks += [jnp.sum(row_z, axis=0, keepdims=True) * same_y, row_z]
        picks = jnp.concatenate(picks, axis=0).astype(BF)
        counts = jnp.dot(picks, ones, preferred_element_type=F32)
        for x in range(rows):
            pick = slice(x * both, (x + 1) * both)
            cells_x = feat_ref[x, pl.ds(first, tile_y)].reshape(cells, chans)
            sums = jnp.dot(picks[pick], cells_x, preferred_element_type=F32)
            pool = (sums[:tile_y] * lax.rsqrt(1.0 + counts[pick][:tile_y])).astype(BF)
            for g in range(tile_y // group):
                start = first + g * group
                at = slice(None) if group == ys else pl.ds(pl.multiple_of(start % ys, group), group)
                xy_ref[start // ys, x, at] = pool[g * group : (g + 1) * group]
            xz_acc[x] += sums[tile_y:]
            xz_cnt[x] += counts[pick][tile_y:]

    lax.fori_loop(0, tiles, tile, None)
    xz_ref[...] = (xz_acc[...] * lax.rsqrt(1.0 + xz_cnt[...])).astype(BF)


def pools(feat, by_z, n):
    rows, y_len, zs, chans = feat.shape
    vmem = pl.BlockSpec(memory_space=pltpu.VMEM)
    return pl.pallas_call(
        pool_body,
        in_specs=[vmem] * 2,
        out_specs=[vmem] * 2,
        out_shape=[
            jax.ShapeDtypeStruct((n, rows, y_len // n, chans), BF),
            jax.ShapeDtypeStruct((rows, zs, chans), BF),
        ],
        scratch_shapes=[pltpu.VMEM((rows, zs, chans), F32)] * 2,
        compiler_params=pltpu.CompilerParams(vmem_limit_bytes=8 << 20),
        cost_estimate=pl.CostEstimate(flops=2 * 32 * feat.size, bytes_accessed=1 << 20, transcendentals=0),
        name="pools",
    )(feat, by_z)


def planes_body(xy_ref, xz_ref, xy_in, xy_out, xz_in, xz_out, xy_plane, xz_plane):
    size = min(256, xy_ref.shape[0])
    for r in range(0, xy_ref.shape[0], size):
        xy_plane[r : r + size] = mlp(xy_ref[r : r + size], 0.5 * xy_in[...], xy_out[...])
    xz_plane[...] = mlp(xz_ref[...], 0.5 * xz_in[...], xz_out[...])


def planes(xy_pool, xz_pool, xy_in, xy_out, xz_in, xz_out):
    vmem = pl.BlockSpec(memory_space=pltpu.VMEM)
    flops = 4 * (xy_pool.size + xz_pool.size) * xy_in.shape[1]
    return pl.pallas_call(
        planes_body,
        in_specs=[vmem] * 6,
        out_specs=[vmem] * 2,
        out_shape=[jax.ShapeDtypeStruct(xy_pool.shape, BF), jax.ShapeDtypeStruct(xz_pool.shape, BF)],
        compiler_params=pltpu.CompilerParams(vmem_limit_bytes=8 << 20),
        cost_estimate=pl.CostEstimate(flops=flops, bytes_accessed=1 << 20, transcendentals=0),
        name="planes",
    )(xy_pool, xz_pool, xy_in, xy_out, xz_in, xz_out)


def yz_body(parts, zs, *refs):
    w_in, w_out, out = refs[parts:]
    count, cells, chans = out.shape
    pools = []
    for u in range(count):
        total = refs[0][u].astype(F32)
        for v in range(1, parts):
            total = total + refs[v][u ^ v].astype(F32)
        scale = lax.rsqrt(1.0 + total[cells:])
        pools += [
            total[r : r + zs] * jnp.broadcast_to(scale[:, y : y + 1], (zs, chans))
            for y, r in enumerate(range(0, cells, zs))
        ]
    pool = jnp.concatenate(pools, axis=0).astype(BF)
    out[...] = mlp(pool, 0.5 * w_in[...], w_out[...]).reshape(count, cells, chans)


def yz_mlp(parts, zs, w_in, w_out):
    vmem = pl.BlockSpec(memory_space=pltpu.VMEM)
    count, rows, chans = parts[0].shape
    cells = rows - zs
    return pl.pallas_call(
        functools.partial(yz_body, len(parts), zs),
        in_specs=[vmem] * (len(parts) + 2),
        out_specs=vmem,
        out_shape=jax.ShapeDtypeStruct((count, cells, chans), BF),
        compiler_params=pltpu.CompilerParams(vmem_limit_bytes=8 << 20),
        cost_estimate=pl.CostEstimate(
            flops=4 * count * cells * w_in.size, bytes_accessed=1 << 19, transcendentals=0
        ),
        name="yz_mlp",
    )(*parts, w_in, w_out)


def first_body(feat_ref, xy_ref, xz_ref, w_in, out_ref):
    n, rows, ys, chans = xy_ref.shape
    zs = xz_ref.shape[1]
    half = 0.5 * w_in[...]

    def chunk(c, _):
        for x in range(rows):
            xy = xy_ref[c, x].astype(F32)
            part = feat_ref[x, pl.ds(c * ys, ys)].astype(F32) + xy[:, None, :] + xz_ref[x].astype(F32)[None]
            part = part.reshape(ys * zs, chans).astype(BF)
            out_ref[c, x] = jnp.dot(part, half, preferred_element_type=F32)

    lax.fori_loop(0, n, chunk, None)


def first_layer(feat, xy_plane, xz_plane, w_in):
    n, rows, ys, _ = xy_plane.shape
    vmem = pl.BlockSpec(memory_space=pltpu.VMEM)
    return pl.pallas_call(
        first_body,
        in_specs=[vmem] * 4,
        out_specs=vmem,
        out_shape=jax.ShapeDtypeStruct((n, rows, ys * xz_plane.shape[1], w_in.shape[1]), F32),
        compiler_params=pltpu.CompilerParams(vmem_limit_bytes=8 << 20),
        cost_estimate=pl.CostEstimate(flops=2 * feat.size * w_in.shape[1], bytes_accessed=1 << 20, transcendentals=0),
        name="first_layer",
    )(feat, xy_plane, xz_plane, w_in)


def voxel_body(n, groups, before, last, me_ref, first_ref, w_in, w_out, *refs):
    yz_refs, refs = refs[: len(groups)], refs[len(groups) :]
    if before:
        prev_ref, refs = refs[0], refs[2:]
    out_hbm, done_ref, own_ref, sems = refs
    _, rows, ys, zs, chans = done_ref.shape
    half = 0.5 * w_in[...]

    def send(source, index, pos, sem):
        at = pl.ds((offset(pos, n) ^ me_ref[0]) * ys, ys)
        return pltpu.make_async_copy(source.at[index], out_hbm.at[:, at], sems.at[sem])

    copies = [send(prev_ref, j, pos, j) for j, pos in enumerate(before)]
    for copy in copies:
        copy.start()
    slot = 0
    for yz_ref, (_, count) in zip(yz_refs, groups):
        both = yz_ref[...].reshape(count * ys * zs, chans)
        both = jnp.dot(both, half, preferred_element_type=F32)
        own_ref[slot : slot + count] = both.reshape(count, ys * zs, half.shape[1])
        slot += count
    slot = 0
    for yz_ref, (pos0, count) in zip(yz_refs, groups):

        def chunk(j, _, yz_ref=yz_ref, pos0=pos0, slot=slot):
            home = offset(pos0 + j, n) ^ me_ref[0]
            for x in range(0, rows, 3):
                hidden = silu(first_ref[home, x : x + 3] + own_ref[slot + j][None]).astype(BF)
                cells = jnp.dot(hidden.reshape(3 * ys * zs, -1), w_out[...], preferred_element_type=F32).astype(BF)
                done_ref[slot + j, x : x + 3] = cells.reshape(3, ys, zs, chans)
            if last:
                send(done_ref, slot + j, pos0 + j, len(before) + slot + j).start()

        lax.fori_loop(0, count, chunk, None)
        slot += count
    if last:
        slot = 0
        for pos0, count in groups:
            copies += [send(done_ref, slot + j, pos0 + j, len(before) + slot + j) for j in range(count)]
            slot += count
    for copy in copies:
        copy.wait()


def voxels(state, n, groups, yz, last, me, shape, first, w_in, w_out):
    rows, y_len, zs, chans = shape
    ys, size = y_len // n, sum(count for _, count in groups)
    before, extra = ([], []) if state is None else (state[0], list(state[1:]))
    vmem = pl.BlockSpec(memory_space=pltpu.VMEM)
    hbm = pl.BlockSpec(memory_space=pltpu.MemorySpace.HBM)
    done = (size, rows, ys, zs, chans)
    operands = [me.reshape(1), first, w_in, w_out, *yz, *extra]
    sems = pltpu.SemaphoreType.DMA((len(before) + (size if last else 0) or 1,))
    out = pl.pallas_call(
        functools.partial(voxel_body, n, groups, before, last),
        in_specs=[pl.BlockSpec(memory_space=pltpu.SMEM)] + [vmem] * (3 + len(yz)) + [vmem, hbm][: len(extra)],
        out_specs=[hbm] if last else [hbm, vmem],
        out_shape=[jax.ShapeDtypeStruct(shape, BF)] + ([] if last else [jax.ShapeDtypeStruct(done, BF)]),
        scratch_shapes=([pltpu.VMEM(done, BF)] if last else [])
        + [pltpu.VMEM((size, ys * zs, w_in.shape[1]), F32), sems],
        input_output_aliases={len(operands) - 1: 0} if extra else {},
        compiler_params=pltpu.CompilerParams(vmem_limit_bytes=20 << 20, has_side_effects=True),
        cost_estimate=pl.CostEstimate(
            flops=4 * size * rows * ys * zs * w_in.size, bytes_accessed=1 << 20, transcendentals=0
        ),
        name="voxels",
    )(*operands)
    if last:
        return out[0]
    return [pos0 + j for pos0, count in groups for j in range(count)], out[1], out[0]


def swap(value, n, offset):
    return lax.ppermute(value, "gx", [(i, i ^ offset) for i in range(n)])


def per_device(n, features, occupancy, heights, xy_in, xy_out, xz_in, xz_out, yz_in, yz_out, voxel_in, voxel_out):
    zs = features.shape[2]
    me = lax.axis_index("gx")
    parts, by_z, feat = partials(features, jnp.swapaxes(occupancy, 1, 2), heights, me, n)
    chans = features.shape[3]

    digits = radices(n)
    weights = [1]
    for digit in digits:
        weights.append(weights[-1] * digit)
    held = parts
    for stage, digit in enumerate(digits[:-1]):
        size = held.shape[0] // digit
        pieces = [held[:size]] + [
            swap(held[d * size : (d + 1) * size], n, mask(d, weights[stage])) for d in range(1, digit)
        ]
        if stage == 1:
            pieces, xy_plane, xz_plane = lax.optimization_barrier((pieces, xy_plane, xz_plane))
        held = sum(piece.astype(F32) for piece in pieces).astype(BF)
        if stage == 0:
            held, by_z = lax.optimization_barrier((held, by_z))
            xy_pool, xz_pool = pools(feat, by_z, n)
            xy_plane, xz_plane = planes(
                xy_pool.reshape(-1, chans), xz_pool.reshape(-1, chans), xy_in, xy_out, xz_in, xz_out
            )
    first = first_layer(feat, xy_plane.reshape(xy_pool.shape), xz_plane.reshape(xz_pool.shape), voxel_in)
    slower = digits[-1]
    pieces = [held] + [swap(held, n, mask(d, weights[len(digits) - 1])) for d in range(1, slower)]
    pieces, first = lax.optimization_barrier((pieces, first))
    plane = yz_mlp(pieces, zs, yz_in, yz_out)

    call = functools.partial(voxels, me=me, shape=features.shape, first=first, w_in=voxel_in, w_out=voxel_out)
    sibling = n // 2
    passed = swap(plane, n, 1)
    state = call(None, n, [(0, slower)], [plane], False)
    state = call(state, n, [(sibling, slower)], [passed], False)
    waiting = []
    for stage, digit in reversed(list(enumerate(digits))[1:-1]):
        arrived = []
        for d in range(1, digit):
            arrived.append(swap(plane, n, mask(d, weights[stage])))
        for d, piece in enumerate(arrived, 1):
            piece, *tail = lax.optimization_barrier((piece, *state[1:]))
            state = (state[0], *tail)
            pieces = waiting + [((d * slower, slower), piece)]
            waiting = [((sibling + d * slower, slower), swap(piece, n, 1))]
            state = call(state, n, [g for g, _ in pieces], [p for _, p in pieces], False)
        plane = jnp.concatenate([plane] + arrived, axis=0)
        slower *= digit
    return call(state, n, [g for g, _ in waiting], [p for _, p in waiting], True)


def solution(mesh):
    split = ("group", "gx")
    in_specs = (P(split, None, None, None), P(split, None, None), P(split, None)) + (P(),) * 8
    n = mesh.shape["gx"]

    def body(*args):
        return per_device(n, *args)

    step = jax.shard_map(
        body, mesh=mesh, in_specs=in_specs, out_specs=P(split, None, None, None), check_vma=False
    )
    if len(radices(n)) > 3:
        return step
    return step
```

```python
import functools

import jax
import jax.numpy as jnp
from jax import lax
from jax.experimental import pallas as pl
from jax.experimental.pallas import tpu as pltpu
from jax.sharding import PartitionSpec as P


BF = jnp.bfloat16
F32 = jnp.float32


def radices(n):
    digits, left = [2], n // 2
    while left > 1:
        digits.append(4 if left % 4 == 0 else 2)
        left //= digits[-1]
    return digits


def mask(digit, weight):
    return digit * weight ^ (1 if weight == 2 else 0)


def offset(pos, n):
    off, slower, weight = 0, n, 1
    for digit in radices(n):
        slower //= digit
        value = (pos // slower) % digit
        crossed = jnp.minimum(value, 1) if weight == 2 else 0
        off = off ^ (value * weight) ^ crossed
        weight *= digit
    return off


def silu(half):
    return half + half * jnp.tanh(half)


def mlp(x, w_in, w_out):
    hidden = silu(jnp.dot(x, w_in, preferred_element_type=F32)).astype(BF)
    return jnp.dot(hidden, w_out, preferred_element_type=F32).astype(BF)


def position(off, n):
    pos, slower, weight, core = 0, n, 1, off % 2
    for digit in radices(n):
        slower //= digit
        if weight > 1:
            value = (off // weight) % digit
            pos = pos + value * slower
            core = core ^ jnp.minimum(value, 1) if weight == 2 else core
        weight *= digit
    return pos + core * (n // 2)


def sum_tiles(n, split, pos0, me, feat_ref, by_cell_ref, seen_ref, part_ref, even_ref, odd_ref, wait):
    rows, y_len, zs, chans = feat_ref.shape
    ys = y_len // n
    tiles, cells, stack = by_cell_ref.shape
    tile_y, lanes = cells // zs, chans
    group = min(ys, tile_y)
    steps = part_ref.shape[0] if split else tiles
    iota = lambda axis: lax.broadcasted_iota(jnp.int32, (stack, rows * chans), axis)
    widen = (iota(0) // zs == iota(1) // chans).astype(F32).astype(BF)

    def tile_of(i):
        return offset(pos0 + i, n) ^ me if split else i

    def expand(i, wide_ref):
        wide_ref[...] = jnp.dot(by_cell_ref[tile_of(i)], widen, preferred_element_type=F32)

    def tile(i, wide_ref):
        first = tile_of(i) * tile_y
        for g in range(tile_y // group):
            start = first + g * group
            home, inner = i if split else position((start // ys) ^ me, n), start % ys
            for y in range(group):
                cell = (g * group + y) * zs
                total = None
                for x in range(rows):
                    weight = wide_ref[cell : cell + zs, x * chans : (x + 1) * chans]
                    term = feat_ref[x, start + y].astype(F32) * weight
                    total = term if total is None else total + term
                at = y * zs if group == ys else pl.multiple_of((inner + y) * zs, zs)
                part_ref[home, pl.ds(at, zs), :] = total.astype(BF)
            shift = lax.rem(lanes - lax.rem(start - inner, lanes), lanes)
            part_ref[home, ys * zs :, :] = pltpu.roll(seen_ref[start // lanes], shift, 1).astype(BF)

    def pair(p, _):
        i = 2 * p
        wait(tile_of(i))
        wait(tile_of(i + 1))
        expand(i + 1, odd_ref)
        tile(i, even_ref)
        expand(jnp.minimum(i + 2, steps - 1), even_ref)
        tile(i + 1, odd_ref)

    expand(0, even_ref)
    lax.fori_loop(0, steps // 2, pair, None)


def partial_body(
    n, split, me_ref, feat_hbm, occ_hbm, hgt_hbm, part_ref, by_z_ref, feat_ref, by_cell_ref, seen_ref,
    occ_ref, hgt_ref, even_ref, odd_ref, feat_sems, side_sems,
):
    rows, y_len, zs, chans = feat_ref.shape
    tiles, cells, _ = by_cell_ref.shape
    tile_y, lanes, stack = cells // zs, chans, rows * zs
    me = me_ref[0]

    def fetch(t):
        at = pl.ds(t * tile_y, tile_y)
        return pltpu.make_async_copy(feat_hbm.at[:, at], feat_ref.at[:, at], feat_sems.at[t])

    def tile_of(i):
        return offset((i + tiles // 2) % tiles, n) ^ me if split else i

    sides = [
        pltpu.make_async_copy(occ_hbm, occ_ref, side_sems.at[0]),
        pltpu.make_async_copy(hgt_hbm, hgt_ref, side_sems.at[1]),
    ]
    for side in sides:
        side.start()
    lax.fori_loop(0, tiles, lambda i, _: fetch(tile_of(i)).start(), None)

    iota = lambda shape, axis: lax.broadcasted_iota(jnp.int32, shape, axis)
    same_z = (iota((stack, cells), 0) % zs == iota((stack, cells), 1) % zs).astype(F32)
    zidx = iota((zs, lanes), 0)
    parts = lanes // tile_y
    spread = (iota((lanes, parts * cells), 0) == iota((lanes, parts * cells), 1) // zs).astype(F32).astype(BF)
    for side in sides:
        side.wait()

    for block in range(y_len // lanes):
        at = slice(block * lanes, (block + 1) * lanes)
        weights = [
            jnp.where(zidx < hgt_ref[x : x + 1, at], occ_ref[x, :, at], 0).astype(F32) for x in range(rows)
        ]
        seen_ref[block] = sum(weights[1:], weights[0])
        stacked = jnp.concatenate(weights, axis=0).astype(BF)
        for part in range(parts):
            columns = slice(part * cells, (part + 1) * cells)
            by_z_ref[block * parts + part] = (
                jnp.dot(stacked, spread[:, columns], preferred_element_type=F32) * same_z
            )
    for t in range(tiles):
        by_cell_ref[t] = by_z_ref[t].T.astype(BF)
    sum_tiles(
        n, split, n // 2, me, feat_ref, by_cell_ref, seen_ref, part_ref, even_ref, odd_ref, lambda t: fetch(t).wait()
    )
    if split:
        lax.fori_loop(tiles // 2, tiles, lambda i, _: fetch(tile_of(i)).wait(), None)


def own_body(n, me_ref, feat_ref, by_cell_ref, seen_ref, part_ref, even_ref, odd_ref):
    sum_tiles(
        n, True, 0, me_ref[0], feat_ref, by_cell_ref, seen_ref, part_ref, even_ref, odd_ref, lambda t: None
    )


def partials(feat, occ, hgt, me, n):
    rows, y_len, zs, chans = feat.shape
    ys = y_len // n
    tile_y = 256 // zs
    tiles, cells = y_len // tile_y, tile_y * zs
    split = ys == tile_y
    vmem = pl.BlockSpec(memory_space=pltpu.VMEM)
    hbm = pl.BlockSpec(memory_space=pltpu.MemorySpace.HBM)
    smem = pl.BlockSpec(memory_space=pltpu.SMEM)
    block = jax.ShapeDtypeStruct((n // 2 if split else n, ys * zs + zs, chans), BF)
    wide = [pltpu.VMEM((cells, rows * chans), F32)] * 2
    cost = pl.CostEstimate(flops=4 * feat.size, bytes_accessed=feat.size, transcendentals=0)
    part, by_z, kept, by_cell, seen = pl.pallas_call(
        functools.partial(partial_body, n, split),
        in_specs=[smem, hbm, hbm, hbm],
        out_specs=[vmem] * 5,
        out_shape=[
            block,
            jax.ShapeDtypeStruct((tiles, rows * zs, cells), F32),
            jax.ShapeDtypeStruct(feat.shape, BF),
            jax.ShapeDtypeStruct((tiles, cells, rows * zs), BF),
            jax.ShapeDtypeStruct((y_len // chans, zs, chans), F32),
        ],
        scratch_shapes=[pltpu.VMEM(occ.shape, jnp.int32), pltpu.VMEM(hgt.shape, jnp.int32)]
        + wide
        + [pltpu.SemaphoreType.DMA((tiles,)), pltpu.SemaphoreType.DMA((2,))],
        compiler_params=pltpu.CompilerParams(vmem_limit_bytes=16 << 20),
        cost_estimate=cost,
        name="partials",
    )(me.reshape(1), *(pltpu.with_memory_space_constraint(a, pltpu.MemorySpace.HBM) for a in (feat, occ, hgt)))
    if not split:
        return part[n // 2 :], part[: n // 2], by_z, kept
    own = pl.pallas_call(
        functools.partial(own_body, n),
        in_specs=[smem] + [vmem] * 3,
        out_specs=vmem,
        out_shape=block,
        scratch_shapes=wide,
        compiler_params=pltpu.CompilerParams(vmem_limit_bytes=8 << 20),
        cost_estimate=cost,
        name="own_partials",
    )(me.reshape(1), kept, by_cell, seen)
    return part, own, by_z, kept


def pool_body(feat_ref, by_z_ref, xy_ref, xz_ref, xz_acc, xz_cnt):
    rows, _, zs, chans = feat_ref.shape
    _, _, ys, _ = xy_ref.shape
    tiles, _, cells = by_z_ref.shape
    tile_y = cells // zs
    both, group = tile_y + zs, min(ys, tile_y)
    iota = lambda axis: lax.broadcasted_iota(jnp.int32, (tile_y, cells), axis)
    same_y = (iota(0) == iota(1) // zs).astype(F32)
    ones = jnp.ones((cells, chans), BF)
    xz_acc[...] = jnp.zeros_like(xz_acc)
    xz_cnt[...] = jnp.zeros_like(xz_cnt)

    def tile(t, _):
        first = t * tile_y
        picks = []
        for x in range(rows):
            row_z = by_z_ref[t, x * zs : (x + 1) * zs]
            picks += [jnp.sum(row_z, axis=0, keepdims=True) * same_y, row_z]
        picks = jnp.concatenate(picks, axis=0).astype(BF)
        counts = jnp.dot(picks, ones, preferred_element_type=F32)
        for x in range(rows):
            pick = slice(x * both, (x + 1) * both)
            cells_x = feat_ref[x, pl.ds(first, tile_y)].reshape(cells, chans)
            sums = jnp.dot(picks[pick], cells_x, preferred_element_type=F32)
            pool = (sums[:tile_y] * lax.rsqrt(1.0 + counts[pick][:tile_y])).astype(BF)
            for g in range(tile_y // group):
                start = first + g * group
                at = slice(None) if group == ys else pl.ds(pl.multiple_of(start % ys, group), group)
                xy_ref[start // ys, x, at] = pool[g * group : (g + 1) * group]
            xz_acc[x] += sums[tile_y:]
            xz_cnt[x] += counts[pick][tile_y:]

    lax.fori_loop(0, tiles, tile, None)
    xz_ref[...] = (xz_acc[...] * lax.rsqrt(1.0 + xz_cnt[...])).astype(BF)


def pools(feat, by_z, n):
    rows, y_len, zs, chans = feat.shape
    vmem = pl.BlockSpec(memory_space=pltpu.VMEM)
    return pl.pallas_call(
        pool_body,
        in_specs=[vmem] * 2,
        out_specs=[vmem] * 2,
        out_shape=[
            jax.ShapeDtypeStruct((n, rows, y_len // n, chans), BF),
            jax.ShapeDtypeStruct((rows, zs, chans), BF),
        ],
        scratch_shapes=[pltpu.VMEM((rows, zs, chans), F32)] * 2,
        compiler_params=pltpu.CompilerParams(vmem_limit_bytes=8 << 20),
        cost_estimate=pl.CostEstimate(flops=2 * 32 * feat.size, bytes_accessed=1 << 20, transcendentals=0),
        name="pools",
    )(feat, by_z)


def planes_body(xy_ref, xz_ref, xy_in, xy_out, xz_in, xz_out, xy_plane, xz_plane):
    size = min(256, xy_ref.shape[0])
    for r in range(0, xy_ref.shape[0], size):
        xy_plane[r : r + size] = mlp(xy_ref[r : r + size], 0.5 * xy_in[...], xy_out[...])
    xz_plane[...] = mlp(xz_ref[...], 0.5 * xz_in[...], xz_out[...])


def planes(xy_pool, xz_pool, xy_in, xy_out, xz_in, xz_out):
    vmem = pl.BlockSpec(memory_space=pltpu.VMEM)
    flops = 4 * (xy_pool.size + xz_pool.size) * xy_in.shape[1]
    return pl.pallas_call(
        planes_body,
        in_specs=[vmem] * 6,
        out_specs=[vmem] * 2,
        out_shape=[jax.ShapeDtypeStruct(xy_pool.shape, BF), jax.ShapeDtypeStruct(xz_pool.shape, BF)],
        compiler_params=pltpu.CompilerParams(vmem_limit_bytes=8 << 20),
        cost_estimate=pl.CostEstimate(flops=flops, bytes_accessed=1 << 20, transcendentals=0),
        name="planes",
    )(xy_pool, xz_pool, xy_in, xy_out, xz_in, xz_out)


def yz_body(parts, zs, *refs):
    w_in, w_out, out = refs[parts:]
    count, cells, chans = out.shape
    pools = []
    for u in range(count):
        total = refs[0][u].astype(F32)
        for v in range(1, parts):
            total = total + refs[v][u ^ v].astype(F32)
        scale = lax.rsqrt(1.0 + total[cells:])
        pools += [
            total[r : r + zs] * jnp.broadcast_to(scale[:, y : y + 1], (zs, chans))
            for y, r in enumerate(range(0, cells, zs))
        ]
    pool = jnp.concatenate(pools, axis=0).astype(BF)
    out[...] = mlp(pool, 0.5 * w_in[...], w_out[...]).reshape(count, cells, chans)


def yz_mlp(parts, zs, w_in, w_out):
    vmem = pl.BlockSpec(memory_space=pltpu.VMEM)
    count, rows, chans = parts[0].shape
    cells = rows - zs
    return pl.pallas_call(
        functools.partial(yz_body, len(parts), zs),
        in_specs=[vmem] * (len(parts) + 2),
        out_specs=vmem,
        out_shape=jax.ShapeDtypeStruct((count, cells, chans), BF),
        compiler_params=pltpu.CompilerParams(vmem_limit_bytes=8 << 20),
        cost_estimate=pl.CostEstimate(
            flops=4 * count * cells * w_in.size, bytes_accessed=1 << 19, transcendentals=0
        ),
        name="yz_mlp",
    )(*parts, w_in, w_out)


def first_body(feat_ref, xy_ref, xz_ref, w_in, out_ref):
    n, rows, ys, chans = xy_ref.shape
    zs = xz_ref.shape[1]
    half = 0.5 * w_in[...]

    def chunk(c, _):
        for x in range(rows):
            xy = xy_ref[c, x].astype(F32)
            part = feat_ref[x, pl.ds(c * ys, ys)].astype(F32) + xy[:, None, :] + xz_ref[x].astype(F32)[None]
            part = part.reshape(ys * zs, chans).astype(BF)
            out_ref[c, x] = jnp.dot(part, half, preferred_element_type=F32)

    lax.fori_loop(0, n, chunk, None)


def first_layer(feat, xy_plane, xz_plane, w_in):
    n, rows, ys, _ = xy_plane.shape
    vmem = pl.BlockSpec(memory_space=pltpu.VMEM)
    return pl.pallas_call(
        first_body,
        in_specs=[vmem] * 4,
        out_specs=vmem,
        out_shape=jax.ShapeDtypeStruct((n, rows, ys * xz_plane.shape[1], w_in.shape[1]), F32),
        compiler_params=pltpu.CompilerParams(vmem_limit_bytes=8 << 20),
        cost_estimate=pl.CostEstimate(flops=2 * feat.size * w_in.shape[1], bytes_accessed=1 << 20, transcendentals=0),
        name="first_layer",
    )(feat, xy_plane, xz_plane, w_in)


def voxel_body(n, groups, before, last, me_ref, first_ref, w_in, w_out, *refs):
    yz_refs, refs = refs[: len(groups)], refs[len(groups) :]
    if before:
        prev_ref, refs = refs[0], refs[2:]
    out_hbm, done_ref, own_ref, sems = refs
    _, rows, ys, zs, chans = done_ref.shape
    half = 0.5 * w_in[...]

    def send(source, index, pos, sem):
        at = pl.ds((offset(pos, n) ^ me_ref[0]) * ys, ys)
        return pltpu.make_async_copy(source.at[index], out_hbm.at[:, at], sems.at[sem])

    copies = [send(prev_ref, j, pos, j) for j, pos in enumerate(before)]
    for copy in copies:
        copy.start()
    slot = 0
    for yz_ref, (_, count) in zip(yz_refs, groups):
        both = yz_ref[...].reshape(count * ys * zs, chans)
        both = jnp.dot(both, half, preferred_element_type=F32)
        own_ref[slot : slot + count] = both.reshape(count, ys * zs, half.shape[1])
        slot += count
    slot = 0
    for yz_ref, (pos0, count) in zip(yz_refs, groups):

        def chunk(j, _, yz_ref=yz_ref, pos0=pos0, slot=slot):
            home = offset(pos0 + j, n) ^ me_ref[0]
            for x in range(0, rows, 3):
                hidden = silu(first_ref[home, x : x + 3] + own_ref[slot + j][None]).astype(BF)
                cells = jnp.dot(hidden.reshape(3 * ys * zs, -1), w_out[...], preferred_element_type=F32).astype(BF)
                done_ref[slot + j, x : x + 3] = cells.reshape(3, ys, zs, chans)
            if last:
                send(done_ref, slot + j, pos0 + j, len(before) + slot + j).start()

        lax.fori_loop(0, count, chunk, None)
        slot += count
    if last:
        slot = 0
        for pos0, count in groups:
            copies += [send(done_ref, slot + j, pos0 + j, len(before) + slot + j) for j in range(count)]
            slot += count
    for copy in copies:
        copy.wait()


def voxels(state, n, groups, yz, last, me, shape, first, w_in, w_out):
    rows, y_len, zs, chans = shape
    ys, size = y_len // n, sum(count for _, count in groups)
    before, extra = ([], []) if state is None else (state[0], list(state[1:]))
    vmem = pl.BlockSpec(memory_space=pltpu.VMEM)
    hbm = pl.BlockSpec(memory_space=pltpu.MemorySpace.HBM)
    done = (size, rows, ys, zs, chans)
    operands = [me.reshape(1), first, w_in, w_out, *yz, *extra]
    sems = pltpu.SemaphoreType.DMA((len(before) + (size if last else 0) or 1,))
    out = pl.pallas_call(
        functools.partial(voxel_body, n, groups, before, last),
        in_specs=[pl.BlockSpec(memory_space=pltpu.SMEM)] + [vmem] * (3 + len(yz)) + [vmem, hbm][: len(extra)],
        out_specs=[hbm] if last else [hbm, vmem],
        out_shape=[jax.ShapeDtypeStruct(shape, BF)] + ([] if last else [jax.ShapeDtypeStruct(done, BF)]),
        scratch_shapes=([pltpu.VMEM(done, BF)] if last else [])
        + [pltpu.VMEM((size, ys * zs, w_in.shape[1]), F32), sems],
        input_output_aliases={len(operands) - 1: 0} if extra else {},
        compiler_params=pltpu.CompilerParams(vmem_limit_bytes=20 << 20, has_side_effects=True),
        cost_estimate=pl.CostEstimate(
            flops=4 * size * rows * ys * zs * w_in.size, bytes_accessed=1 << 20, transcendentals=0
        ),
        name="voxels",
    )(*operands)
    if last:
        return out[0]
    return [pos0 + j for pos0, count in groups for j in range(count)], out[1], out[0]


def swap(value, n, offset):
    return lax.ppermute(value, "gx", [(i, i ^ offset) for i in range(n)])


def per_device(n, features, occupancy, heights, xy_in, xy_out, xz_in, xz_out, yz_in, yz_out, voxel_in, voxel_out):
    zs = features.shape[2]
    me = lax.axis_index("gx")
    theirs, held, by_z, feat = partials(features, jnp.swapaxes(occupancy, 1, 2), heights, me, n)
    chans = features.shape[3]

    digits = radices(n)
    weights = [1]
    for digit in digits:
        weights.append(weights[-1] * digit)
    for stage, digit in enumerate(digits[:-1]):
        size = held.shape[0] // digit
        if stage == 0:
            pieces = [held, swap(theirs, n, 1)]
        else:
            pieces = [held[:size]] + [
                swap(held[d * size : (d + 1) * size], n, mask(d, weights[stage])) for d in range(1, digit)
            ]
        if stage == 1:
            pieces, xy_plane, xz_plane = lax.optimization_barrier((pieces, xy_plane, xz_plane))
        held = sum(piece.astype(F32) for piece in pieces).astype(BF)
        if stage == 0:
            held, by_z = lax.optimization_barrier((held, by_z))
            xy_pool, xz_pool = pools(feat, by_z, n)
            xy_plane, xz_plane = planes(
                xy_pool.reshape(-1, chans), xz_pool.reshape(-1, chans), xy_in, xy_out, xz_in, xz_out
            )
    first = first_layer(feat, xy_plane.reshape(xy_pool.shape), xz_plane.reshape(xz_pool.shape), voxel_in)
    slower = digits[-1]
    pieces = [held] + [swap(held, n, mask(d, weights[len(digits) - 1])) for d in range(1, slower)]
    pieces, first = lax.optimization_barrier((pieces, first))
    plane = yz_mlp(pieces, zs, yz_in, yz_out)

    call = functools.partial(voxels, me=me, shape=features.shape, first=first, w_in=voxel_in, w_out=voxel_out)
    sibling = n // 2
    passed = swap(plane, n, 1)
    state = call(None, n, [(0, slower)], [plane], False)
    state = call(state, n, [(sibling, slower)], [passed], False)
    waiting = []
    for stage, digit in reversed(list(enumerate(digits))[1:-1]):
        arrived = []
        for d in range(1, digit):
            arrived.append(swap(plane, n, mask(d, weights[stage])))
        for d, piece in enumerate(arrived, 1):
            piece, *tail = lax.optimization_barrier((piece, *state[1:]))
            state = (state[0], *tail)
            pieces = waiting + [((d * slower, slower), piece)]
            waiting = [((sibling + d * slower, slower), swap(piece, n, 1))]
            state = call(state, n, [g for g, _ in pieces], [p for _, p in pieces], False)
        plane = jnp.concatenate([plane] + arrived, axis=0)
        slower *= digit
    return call(state, n, [g for g, _ in waiting], [p for _, p in waiting], True)


def solution(mesh):
    split = ("group", "gx")
    in_specs = (P(split, None, None, None), P(split, None, None), P(split, None)) + (P(),) * 8
    n = mesh.shape["gx"]

    def body(*args):
        return per_device(n, *args)

    step = jax.shard_map(
        body, mesh=mesh, in_specs=in_specs, out_specs=P(split, None, None, None), check_vma=False
    )
    if len(radices(n)) > 3:
        return step
    return step
```

```python
import functools

import jax
import jax.numpy as jnp
from jax import lax
from jax.experimental import pallas as pl
from jax.experimental.pallas import tpu as pltpu
from jax.sharding import PartitionSpec as P


BF = jnp.bfloat16
F32 = jnp.float32


def radices(n):
    digits, left = [2], n // 2
    while left > 1:
        digits.append(4 if left % 4 == 0 else 2)
        left //= digits[-1]
    return digits


def mask(digit, weight):
    return digit * weight ^ (1 if weight == 2 else 0)


def offset(pos, n):
    off, slower, weight = 0, n, 1
    for digit in radices(n):
        slower //= digit
        value = (pos // slower) % digit
        crossed = jnp.minimum(value, 1) if weight == 2 else 0
        off = off ^ (value * weight) ^ crossed
        weight *= digit
    return off


def silu(half):
    return half + half * jnp.tanh(half)


def mlp(x, w_in, w_out):
    hidden = silu(jnp.dot(x, w_in, preferred_element_type=F32)).astype(BF)
    return jnp.dot(hidden, w_out, preferred_element_type=F32).astype(BF)


def position(off, n):
    pos, slower, weight, core = 0, n, 1, off % 2
    for digit in radices(n):
        slower //= digit
        if weight > 1:
            value = (off // weight) % digit
            pos = pos + value * slower
            core = core ^ jnp.minimum(value, 1) if weight == 2 else core
        weight *= digit
    return pos + core * (n // 2)


def sum_tiles(n, split, pos0, me, feat_ref, by_cell_ref, seen_ref, part_ref, even_ref, odd_ref, wait):
    rows, y_len, zs, chans = feat_ref.shape
    ys = y_len // n
    tiles, cells, stack = by_cell_ref.shape
    tile_y, lanes = cells // zs, chans
    group = min(ys, tile_y)
    share = radices(n)[-1]
    block = share * ys * zs
    steps = part_ref.shape[0] * share if split else tiles
    iota = lambda axis: lax.broadcasted_iota(jnp.int32, (stack, rows * chans), axis)
    widen = (iota(0) // zs == iota(1) // chans).astype(F32).astype(BF)

    def tile_of(i):
        return offset(pos0 + i, n) ^ me if split else i

    def expand(i, wide_ref):
        wide_ref[...] = jnp.dot(by_cell_ref[tile_of(i)], widen, preferred_element_type=F32)

    def tile(i, wide_ref):
        first = tile_of(i) * tile_y
        for g in range(tile_y // group):
            start = first + g * group
            home, inner = i if split else position((start // ys) ^ me, n), start % ys
            sub = home % share
            base = sub * ys * zs + (0 if group == ys else inner * zs)
            for y in range(group):
                cell = (g * group + y) * zs
                total = None
                for x in range(rows):
                    weight = wide_ref[cell : cell + zs, x * chans : (x + 1) * chans]
                    term = feat_ref[x, start + y].astype(F32) * weight
                    total = term if total is None else total + term
                at = pl.multiple_of(base + y * zs, zs)
                part_ref[home // share, pl.ds(at, zs), :] = total.astype(BF)
            shift = lax.rem(2 * lanes + sub * ys - lax.rem(start - inner, lanes), lanes)
            counts = pltpu.roll(seen_ref[start // lanes], shift, 1)
            kept = part_ref[home // share, block:, :].astype(F32)
            counts = jnp.where(lax.broadcasted_iota(jnp.int32, counts.shape, 1) // ys == sub, counts, kept)
            part_ref[home // share, block:, :] = counts.astype(BF)

    def pair(p, _):
        i = 2 * p
        wait(tile_of(i))
        wait(tile_of(i + 1))
        expand(i + 1, odd_ref)
        tile(i, even_ref)
        expand(jnp.minimum(i + 2, steps - 1), even_ref)
        tile(i + 1, odd_ref)

    expand(0, even_ref)
    lax.fori_loop(0, steps // 2, pair, None)


def partial_body(
    n, split, me_ref, feat_hbm, occ_hbm, hgt_hbm, part_ref, by_z_ref, feat_ref, by_cell_ref, seen_ref,
    occ_ref, hgt_ref, even_ref, odd_ref, feat_sems, side_sems,
):
    rows, y_len, zs, chans = feat_ref.shape
    tiles, cells, _ = by_cell_ref.shape
    tile_y, lanes, stack = cells // zs, chans, rows * zs
    me = me_ref[0]

    def fetch(t):
        at = pl.ds(t * tile_y, tile_y)
        return pltpu.make_async_copy(feat_hbm.at[:, at], feat_ref.at[:, at], feat_sems.at[t])

    def tile_of(i):
        return offset((i + tiles // 2) % tiles, n) ^ me if split else i

    sides = [
        pltpu.make_async_copy(occ_hbm, occ_ref, side_sems.at[0]),
        pltpu.make_async_copy(hgt_hbm, hgt_ref, side_sems.at[1]),
    ]
    for side in sides:
        side.start()
    lax.fori_loop(0, tiles, lambda i, _: fetch(tile_of(i)).start(), None)

    iota = lambda shape, axis: lax.broadcasted_iota(jnp.int32, shape, axis)
    same_z = (iota((stack, cells), 0) % zs == iota((stack, cells), 1) % zs).astype(F32)
    zidx = iota((zs, lanes), 0)
    parts = lanes // tile_y
    spread = (iota((lanes, parts * cells), 0) == iota((lanes, parts * cells), 1) // zs).astype(F32).astype(BF)
    for side in sides:
        side.wait()

    for block in range(y_len // lanes):
        at = slice(block * lanes, (block + 1) * lanes)
        weights = [
            jnp.where(zidx < hgt_ref[x : x + 1, at], occ_ref[x, :, at], 0).astype(F32) for x in range(rows)
        ]
        seen_ref[block] = sum(weights[1:], weights[0])
        stacked = jnp.concatenate(weights, axis=0).astype(BF)
        for part in range(parts):
            columns = slice(part * cells, (part + 1) * cells)
            by_z_ref[block * parts + part] = (
                jnp.dot(stacked, spread[:, columns], preferred_element_type=F32) * same_z
            )
    for t in range(tiles):
        by_cell_ref[t] = by_z_ref[t].T.astype(BF)
    sum_tiles(
        n, split, n // 2, me, feat_ref, by_cell_ref, seen_ref, part_ref, even_ref, odd_ref, lambda t: fetch(t).wait()
    )
    if split:
        lax.fori_loop(tiles // 2, tiles, lambda i, _: fetch(tile_of(i)).wait(), None)


def own_body(n, me_ref, feat_ref, by_cell_ref, seen_ref, part_ref, even_ref, odd_ref):
    sum_tiles(
        n, True, 0, me_ref[0], feat_ref, by_cell_ref, seen_ref, part_ref, even_ref, odd_ref, lambda t: None
    )


def partials(feat, occ, hgt, me, n):
    rows, y_len, zs, chans = feat.shape
    ys = y_len // n
    tile_y = 256 // zs
    tiles, cells = y_len // tile_y, tile_y * zs
    split = ys == tile_y
    vmem = pl.BlockSpec(memory_space=pltpu.VMEM)
    hbm = pl.BlockSpec(memory_space=pltpu.MemorySpace.HBM)
    smem = pl.BlockSpec(memory_space=pltpu.SMEM)
    share = radices(n)[-1]
    block = jax.ShapeDtypeStruct(((n // 2 if split else n) // share, share * ys * zs + zs, chans), BF)
    wide = [pltpu.VMEM((cells, rows * chans), F32)] * 2
    cost = pl.CostEstimate(flops=4 * feat.size, bytes_accessed=feat.size, transcendentals=0)
    part, by_z, kept, by_cell, seen = pl.pallas_call(
        functools.partial(partial_body, n, split),
        in_specs=[smem, hbm, hbm, hbm],
        out_specs=[vmem] * 5,
        out_shape=[
            block,
            jax.ShapeDtypeStruct((tiles, rows * zs, cells), F32),
            jax.ShapeDtypeStruct(feat.shape, BF),
            jax.ShapeDtypeStruct((tiles, cells, rows * zs), BF),
            jax.ShapeDtypeStruct((y_len // chans, zs, chans), F32),
        ],
        scratch_shapes=[pltpu.VMEM(occ.shape, jnp.int32), pltpu.VMEM(hgt.shape, jnp.int32)]
        + wide
        + [pltpu.SemaphoreType.DMA((tiles,)), pltpu.SemaphoreType.DMA((2,))],
        compiler_params=pltpu.CompilerParams(vmem_limit_bytes=16 << 20),
        cost_estimate=cost,
        name="partials",
    )(me.reshape(1), *(pltpu.with_memory_space_constraint(a, pltpu.MemorySpace.HBM) for a in (feat, occ, hgt)))
    if not split:
        return part[part.shape[0] // 2 :], part[: part.shape[0] // 2], by_z, kept
    own = pl.pallas_call(
        functools.partial(own_body, n),
        in_specs=[smem] + [vmem] * 3,
        out_specs=vmem,
        out_shape=block,
        scratch_shapes=wide,
        compiler_params=pltpu.CompilerParams(vmem_limit_bytes=8 << 20),
        cost_estimate=cost,
        name="own_partials",
    )(me.reshape(1), kept, by_cell, seen)
    return part, own, by_z, kept


def pool_body(feat_ref, by_z_ref, xy_ref, xz_ref, xz_acc, xz_cnt):
    rows, _, zs, chans = feat_ref.shape
    _, _, ys, _ = xy_ref.shape
    tiles, _, cells = by_z_ref.shape
    tile_y = cells // zs
    both, group = tile_y + zs, min(ys, tile_y)
    iota = lambda axis: lax.broadcasted_iota(jnp.int32, (tile_y, cells), axis)
    same_y = (iota(0) == iota(1) // zs).astype(F32)
    ones = jnp.ones((cells, chans), BF)
    xz_acc[...] = jnp.zeros_like(xz_acc)
    xz_cnt[...] = jnp.zeros_like(xz_cnt)

    def tile(t, _):
        first = t * tile_y
        picks = []
        for x in range(rows):
            row_z = by_z_ref[t, x * zs : (x + 1) * zs]
            picks += [jnp.sum(row_z, axis=0, keepdims=True) * same_y, row_z]
        picks = jnp.concatenate(picks, axis=0).astype(BF)
        counts = jnp.dot(picks, ones, preferred_element_type=F32)
        for x in range(rows):
            pick = slice(x * both, (x + 1) * both)
            cells_x = feat_ref[x, pl.ds(first, tile_y)].reshape(cells, chans)
            sums = jnp.dot(picks[pick], cells_x, preferred_element_type=F32)
            pool = (sums[:tile_y] * lax.rsqrt(1.0 + counts[pick][:tile_y])).astype(BF)
            for g in range(tile_y // group):
                start = first + g * group
                at = slice(None) if group == ys else pl.ds(pl.multiple_of(start % ys, group), group)
                xy_ref[start // ys, x, at] = pool[g * group : (g + 1) * group]
            xz_acc[x] += sums[tile_y:]
            xz_cnt[x] += counts[pick][tile_y:]

    lax.fori_loop(0, tiles, tile, None)
    xz_ref[...] = (xz_acc[...] * lax.rsqrt(1.0 + xz_cnt[...])).astype(BF)


def pools(feat, by_z, n):
    rows, y_len, zs, chans = feat.shape
    vmem = pl.BlockSpec(memory_space=pltpu.VMEM)
    return pl.pallas_call(
        pool_body,
        in_specs=[vmem] * 2,
        out_specs=[vmem] * 2,
        out_shape=[
            jax.ShapeDtypeStruct((n, rows, y_len // n, chans), BF),
            jax.ShapeDtypeStruct((rows, zs, chans), BF),
        ],
        scratch_shapes=[pltpu.VMEM((rows, zs, chans), F32)] * 2,
        compiler_params=pltpu.CompilerParams(vmem_limit_bytes=8 << 20),
        cost_estimate=pl.CostEstimate(flops=2 * 32 * feat.size, bytes_accessed=1 << 20, transcendentals=0),
        name="pools",
    )(feat, by_z)


def planes_body(xy_ref, xz_ref, xy_in, xy_out, xz_in, xz_out, xy_plane, xz_plane):
    size = min(256, xy_ref.shape[0])
    for r in range(0, xy_ref.shape[0], size):
        xy_plane[r : r + size] = mlp(xy_ref[r : r + size], 0.5 * xy_in[...], xy_out[...])
    xz_plane[...] = mlp(xz_ref[...], 0.5 * xz_in[...], xz_out[...])


def planes(xy_pool, xz_pool, xy_in, xy_out, xz_in, xz_out):
    vmem = pl.BlockSpec(memory_space=pltpu.VMEM)
    flops = 4 * (xy_pool.size + xz_pool.size) * xy_in.shape[1]
    return pl.pallas_call(
        planes_body,
        in_specs=[vmem] * 6,
        out_specs=[vmem] * 2,
        out_shape=[jax.ShapeDtypeStruct(xy_pool.shape, BF), jax.ShapeDtypeStruct(xz_pool.shape, BF)],
        compiler_params=pltpu.CompilerParams(vmem_limit_bytes=8 << 20),
        cost_estimate=pl.CostEstimate(flops=flops, bytes_accessed=1 << 20, transcendentals=0),
        name="planes",
    )(xy_pool, xz_pool, xy_in, xy_out, xz_in, xz_out)


def yz_body(parts, zs, *refs):
    w_in, w_out, out = refs[parts:]
    count, cells, chans = out.shape
    pools = []
    ys = cells // zs
    for u in range(count):
        total, seen = 0.0, 0.0
        for v in range(parts):
            at = (u ^ v) * cells
            total = total + refs[v][0, at : at + cells].astype(F32)
            seen = seen + refs[v][0, count * cells :, (u ^ v) * ys : (u ^ v) * ys + ys].astype(F32)
        scale = lax.rsqrt(1.0 + seen)
        pools += [
            total[y * zs : (y + 1) * zs] * jnp.broadcast_to(scale[:, y : y + 1], (zs, chans)) for y in range(ys)
        ]
    pool = jnp.concatenate(pools, axis=0).astype(BF)
    out[...] = mlp(pool, 0.5 * w_in[...], w_out[...]).reshape(count, cells, chans)


def yz_mlp(parts, zs, w_in, w_out):
    vmem = pl.BlockSpec(memory_space=pltpu.VMEM)
    count, chans = len(parts), parts[0].shape[2]
    cells = (parts[0].shape[1] - zs) // count
    return pl.pallas_call(
        functools.partial(yz_body, len(parts), zs),
        in_specs=[vmem] * (len(parts) + 2),
        out_specs=vmem,
        out_shape=jax.ShapeDtypeStruct((count, cells, chans), BF),
        compiler_params=pltpu.CompilerParams(vmem_limit_bytes=8 << 20),
        cost_estimate=pl.CostEstimate(
            flops=4 * count * cells * w_in.size, bytes_accessed=1 << 19, transcendentals=0
        ),
        name="yz_mlp",
    )(*parts, w_in, w_out)


def first_body(feat_ref, xy_ref, xz_ref, w_in, out_ref):
    n, rows, ys, chans = xy_ref.shape
    zs = xz_ref.shape[1]
    half = 0.5 * w_in[...]

    def chunk(c, _):
        for x in range(rows):
            xy = xy_ref[c, x].astype(F32)
            part = feat_ref[x, pl.ds(c * ys, ys)].astype(F32) + xy[:, None, :] + xz_ref[x].astype(F32)[None]
            part = part.reshape(ys * zs, chans).astype(BF)
            out_ref[c, x] = jnp.dot(part, half, preferred_element_type=F32)

    lax.fori_loop(0, n, chunk, None)


def first_layer(feat, xy_plane, xz_plane, w_in):
    n, rows, ys, _ = xy_plane.shape
    vmem = pl.BlockSpec(memory_space=pltpu.VMEM)
    return pl.pallas_call(
        first_body,
        in_specs=[vmem] * 4,
        out_specs=vmem,
        out_shape=jax.ShapeDtypeStruct((n, rows, ys * xz_plane.shape[1], w_in.shape[1]), F32),
        compiler_params=pltpu.CompilerParams(vmem_limit_bytes=8 << 20),
        cost_estimate=pl.CostEstimate(flops=2 * feat.size * w_in.shape[1], bytes_accessed=1 << 20, transcendentals=0),
        name="first_layer",
    )(feat, xy_plane, xz_plane, w_in)


def voxel_body(n, groups, before, last, me_ref, first_ref, w_in, w_out, *refs):
    yz_refs, refs = refs[: len(groups)], refs[len(groups) :]
    if before:
        prev_ref, refs = refs[0], refs[2:]
    out_hbm, done_ref, own_ref, sems = refs
    _, rows, ys, zs, chans = done_ref.shape
    half = 0.5 * w_in[...]

    def send(source, index, pos, sem):
        at = pl.ds((offset(pos, n) ^ me_ref[0]) * ys, ys)
        return pltpu.make_async_copy(source.at[index], out_hbm.at[:, at], sems.at[sem])

    copies = [send(prev_ref, j, pos, j) for j, pos in enumerate(before)]
    for copy in copies:
        copy.start()
    slot = 0
    for yz_ref, (_, count) in zip(yz_refs, groups):
        both = yz_ref[...].reshape(count * ys * zs, chans)
        both = jnp.dot(both, half, preferred_element_type=F32)
        own_ref[slot : slot + count] = both.reshape(count, ys * zs, half.shape[1])
        slot += count
    slot = 0
    for yz_ref, (pos0, count) in zip(yz_refs, groups):

        def chunk(j, _, yz_ref=yz_ref, pos0=pos0, slot=slot):
            home = offset(pos0 + j, n) ^ me_ref[0]
            for x in range(0, rows, rows):
                hidden = silu(first_ref[home, x : x + rows] + own_ref[slot + j][None]).astype(BF)
                cells = jnp.dot(hidden.reshape(rows * ys * zs, -1), w_out[...], preferred_element_type=F32).astype(BF)
                done_ref[slot + j, x : x + rows] = cells.reshape(rows, ys, zs, chans)
            if last:
                send(done_ref, slot + j, pos0 + j, len(before) + slot + j).start()

        lax.fori_loop(0, count, chunk, None)
        slot += count
    if last:
        slot = 0
        for pos0, count in groups:
            copies += [send(done_ref, slot + j, pos0 + j, len(before) + slot + j) for j in range(count)]
            slot += count
    for copy in copies:
        copy.wait()


def voxels(state, n, groups, yz, last, me, shape, first, w_in, w_out):
    rows, y_len, zs, chans = shape
    ys, size = y_len // n, sum(count for _, count in groups)
    before, extra = ([], []) if state is None else (state[0], list(state[1:]))
    vmem = pl.BlockSpec(memory_space=pltpu.VMEM)
    hbm = pl.BlockSpec(memory_space=pltpu.MemorySpace.HBM)
    done = (size, rows, ys, zs, chans)
    operands = [me.reshape(1), first, w_in, w_out, *yz, *extra]
    sems = pltpu.SemaphoreType.DMA((len(before) + (size if last else 0) or 1,))
    out = pl.pallas_call(
        functools.partial(voxel_body, n, groups, before, last),
        in_specs=[pl.BlockSpec(memory_space=pltpu.SMEM)] + [vmem] * (3 + len(yz)) + [vmem, hbm][: len(extra)],
        out_specs=[hbm] if last else [hbm, vmem],
        out_shape=[jax.ShapeDtypeStruct(shape, BF)] + ([] if last else [jax.ShapeDtypeStruct(done, BF)]),
        scratch_shapes=([pltpu.VMEM(done, BF)] if last else [])
        + [pltpu.VMEM((size, ys * zs, w_in.shape[1]), F32), sems],
        input_output_aliases={len(operands) - 1: 0} if extra else {},
        compiler_params=pltpu.CompilerParams(vmem_limit_bytes=20 << 20, has_side_effects=True),
        cost_estimate=pl.CostEstimate(
            flops=4 * size * rows * ys * zs * w_in.size, bytes_accessed=1 << 20, transcendentals=0
        ),
        name="voxels",
    )(*operands)
    if last:
        return out[0]
    return [pos0 + j for pos0, count in groups for j in range(count)], out[1], out[0]


def swap(value, n, offset):
    return lax.ppermute(value, "gx", [(i, i ^ offset) for i in range(n)])


def per_device(n, features, occupancy, heights, xy_in, xy_out, xz_in, xz_out, yz_in, yz_out, voxel_in, voxel_out):
    zs = features.shape[2]
    me = lax.axis_index("gx")
    theirs, held, by_z, feat = partials(features, jnp.swapaxes(occupancy, 1, 2), heights, me, n)
    chans = features.shape[3]

    digits = radices(n)
    weights = [1]
    for digit in digits:
        weights.append(weights[-1] * digit)
    for stage, digit in enumerate(digits[:-1]):
        size = held.shape[0] // digit
        if stage == 0:
            pieces = [held, swap(theirs, n, 1)]
        else:
            pieces = [held[:size]] + [
                swap(held[d * size : (d + 1) * size], n, mask(d, weights[stage])) for d in range(1, digit)
            ]
        if stage == 1:
            pieces, xy_plane, xz_plane = lax.optimization_barrier((pieces, xy_plane, xz_plane))
        held = sum(piece.astype(F32) for piece in pieces).astype(BF)
        if stage == 0:
            held, by_z = lax.optimization_barrier((held, by_z))
            xy_pool, xz_pool = pools(feat, by_z, n)
            xy_plane, xz_plane = planes(
                xy_pool.reshape(-1, chans), xz_pool.reshape(-1, chans), xy_in, xy_out, xz_in, xz_out
            )
    first = first_layer(feat, xy_plane.reshape(xy_pool.shape), xz_plane.reshape(xz_pool.shape), voxel_in)
    slower = digits[-1]
    assert held.shape[0] == 1
    pieces = [held] + [swap(held, n, mask(d, weights[len(digits) - 1])) for d in range(1, slower)]
    pieces, first = lax.optimization_barrier((pieces, first))
    plane = yz_mlp(pieces, zs, yz_in, yz_out)

    call = functools.partial(voxels, me=me, shape=features.shape, first=first, w_in=voxel_in, w_out=voxel_out)
    sibling = n // 2
    passed = swap(plane, n, 1)
    state = call(None, n, [(0, slower)], [plane], False)
    state = call(state, n, [(sibling, slower)], [passed], False)
    waiting = []
    for stage, digit in reversed(list(enumerate(digits))[1:-1]):
        arrived = []
        for d in range(1, digit):
            arrived.append(swap(plane, n, mask(d, weights[stage])))
        for d, piece in enumerate(arrived, 1):
            piece, *tail = lax.optimization_barrier((piece, *state[1:]))
            state = (state[0], *tail)
            pieces = waiting + [((d * slower, slower), piece)]
            waiting = [((sibling + d * slower, slower), swap(piece, n, 1))]
            state = call(state, n, [g for g, _ in pieces], [p for _, p in pieces], False)
        plane = jnp.concatenate([plane] + arrived, axis=0)
        slower *= digit
    return call(state, n, [g for g, _ in waiting], [p for _, p in waiting], True)


def solution(mesh):
    split = ("group", "gx")
    in_specs = (P(split, None, None, None), P(split, None, None), P(split, None)) + (P(),) * 8
    n = mesh.shape["gx"]

    def body(*args):
        return per_device(n, *args)

    step = jax.shard_map(
        body, mesh=mesh, in_specs=in_specs, out_specs=P(split, None, None, None), check_vma=False
    )
    if len(radices(n)) > 3:
        return step
    return step
```

```python
import functools

import jax
import jax.numpy as jnp
from jax import lax
from jax.experimental import pallas as pl
from jax.experimental.pallas import tpu as pltpu
from jax.sharding import PartitionSpec as P


BF = jnp.bfloat16
F32 = jnp.float32


def radices(n):
    digits, left = [2], n // 2
    while left > 1:
        digits.append(4 if left % 4 == 0 else 2)
        left //= digits[-1]
    return digits


def mask(digit, weight):
    return digit * weight ^ (1 if weight == 2 else 0)


def offset(pos, n):
    off, slower, weight = 0, n, 1
    for digit in radices(n):
        slower //= digit
        value = (pos // slower) % digit
        crossed = jnp.minimum(value, 1) if weight == 2 else 0
        off = off ^ (value * weight) ^ crossed
        weight *= digit
    return off


def silu(half):
    return half + half * jnp.tanh(half)


def mlp(x, w_in, w_out):
    hidden = silu(jnp.dot(x, w_in, preferred_element_type=F32)).astype(BF)
    return jnp.dot(hidden, w_out, preferred_element_type=F32).astype(BF)


def position(off, n):
    pos, slower, weight, core = 0, n, 1, off % 2
    for digit in radices(n):
        slower //= digit
        if weight > 1:
            value = (off // weight) % digit
            pos = pos + value * slower
            core = core ^ jnp.minimum(value, 1) if weight == 2 else core
        weight *= digit
    return pos + core * (n // 2)


def sum_tiles(n, split, pos0, me, feat_ref, by_cell_ref, seen_ref, part_ref, even_ref, odd_ref, wait):
    rows, y_len, zs, chans = feat_ref.shape
    ys = y_len // n
    tiles, cells, stack = by_cell_ref.shape
    tile_y, lanes = cells // zs, chans
    group = min(ys, tile_y)
    share = radices(n)[-1]
    block = share * ys * zs
    steps = part_ref.shape[0] * share if split else tiles
    iota = lambda axis: lax.broadcasted_iota(jnp.int32, (stack, rows * chans), axis)
    widen = (iota(0) // zs == iota(1) // chans).astype(F32).astype(BF)

    def tile_of(i):
        return offset(pos0 + i, n) ^ me if split else i

    def expand(i, wide_ref):
        wide_ref[...] = jnp.dot(by_cell_ref[tile_of(i)], widen, preferred_element_type=F32)

    def tile(i, wide_ref):
        first = tile_of(i) * tile_y
        for g in range(tile_y // group):
            start = first + g * group
            home, inner = i if split else position((start // ys) ^ me, n), start % ys
            sub = home % share
            base = sub * ys * zs + (0 if group == ys else inner * zs)
            for y in range(group):
                cell = (g * group + y) * zs
                total = None
                for x in range(rows):
                    weight = wide_ref[cell : cell + zs, x * chans : (x + 1) * chans]
                    term = feat_ref[x, start + y].astype(F32) * weight
                    total = term if total is None else total + term
                at = pl.multiple_of(base + y * zs, zs)
                part_ref[home // share, pl.ds(at, zs), :] = total.astype(BF)
            shift = lax.rem(2 * lanes + sub * ys - lax.rem(start - inner, lanes), lanes)
            counts = pltpu.roll(seen_ref[start // lanes], shift, 1)
            kept = part_ref[home // share, block:, :].astype(F32)
            counts = jnp.where(lax.broadcasted_iota(jnp.int32, counts.shape, 1) // ys == sub, counts, kept)
            part_ref[home // share, block:, :] = counts.astype(BF)

    def pair(p, _):
        i = 2 * p
        wait(tile_of(i))
        wait(tile_of(i + 1))
        expand(i + 1, odd_ref)
        tile(i, even_ref)
        expand(jnp.minimum(i + 2, steps - 1), even_ref)
        tile(i + 1, odd_ref)

    expand(0, even_ref)
    lax.fori_loop(0, steps // 2, pair, None)


def partial_body(
    n, split, me_ref, feat_hbm, occ_hbm, hgt_hbm, part_ref, by_z_ref, feat_ref, by_cell_ref, seen_ref,
    occ_ref, hgt_ref, even_ref, odd_ref, feat_sems, side_sems,
):
    rows, y_len, zs, chans = feat_ref.shape
    tiles, cells, _ = by_cell_ref.shape
    tile_y, lanes, stack = cells // zs, chans, rows * zs
    me = me_ref[0]

    def fetch(t):
        at = pl.ds(t * tile_y, tile_y)
        return pltpu.make_async_copy(feat_hbm.at[:, at], feat_ref.at[:, at], feat_sems.at[t])

    def tile_of(i):
        return offset((i + tiles // 2) % tiles, n) ^ me if split else i

    sides = [
        pltpu.make_async_copy(occ_hbm, occ_ref, side_sems.at[0]),
        pltpu.make_async_copy(hgt_hbm, hgt_ref, side_sems.at[1]),
    ]
    for side in sides:
        side.start()
    lax.fori_loop(0, tiles, lambda i, _: fetch(tile_of(i)).start(), None)

    iota = lambda shape, axis: lax.broadcasted_iota(jnp.int32, shape, axis)
    same_z = (iota((stack, cells), 0) % zs == iota((stack, cells), 1) % zs).astype(F32)
    zidx = iota((zs, lanes), 0)
    parts = lanes // tile_y
    spread = (iota((lanes, parts * cells), 0) == iota((lanes, parts * cells), 1) // zs).astype(F32).astype(BF)
    for side in sides:
        side.wait()

    for block in range(y_len // lanes):
        at = slice(block * lanes, (block + 1) * lanes)
        weights = [
            jnp.where(zidx < hgt_ref[x : x + 1, at], occ_ref[x, :, at], 0).astype(F32) for x in range(rows)
        ]
        seen_ref[block] = sum(weights[1:], weights[0])
        stacked = jnp.concatenate(weights, axis=0).astype(BF)
        for part in range(parts):
            columns = slice(part * cells, (part + 1) * cells)
            by_z_ref[block * parts + part] = (
                jnp.dot(stacked, spread[:, columns], preferred_element_type=F32) * same_z
            )
    for t in range(tiles):
        by_cell_ref[t] = by_z_ref[t].T.astype(BF)
    sum_tiles(
        n, split, n // 2, me, feat_ref, by_cell_ref, seen_ref, part_ref, even_ref, odd_ref, lambda t: fetch(t).wait()
    )
    if split:
        lax.fori_loop(tiles // 2, tiles, lambda i, _: fetch(tile_of(i)).wait(), None)


def own_body(n, me_ref, feat_ref, by_cell_ref, seen_ref, part_ref, even_ref, odd_ref):
    sum_tiles(
        n, True, 0, me_ref[0], feat_ref, by_cell_ref, seen_ref, part_ref, even_ref, odd_ref, lambda t: None
    )


def partials(feat, occ, hgt, me, n):
    rows, y_len, zs, chans = feat.shape
    ys = y_len // n
    tile_y = 256 // zs
    tiles, cells = y_len // tile_y, tile_y * zs
    split = ys == tile_y
    vmem = pl.BlockSpec(memory_space=pltpu.VMEM)
    hbm = pl.BlockSpec(memory_space=pltpu.MemorySpace.HBM)
    smem = pl.BlockSpec(memory_space=pltpu.SMEM)
    share = radices(n)[-1]
    block = jax.ShapeDtypeStruct(((n // 2 if split else n) // share, share * ys * zs + zs, chans), BF)
    wide = [pltpu.VMEM((cells, rows * chans), F32)] * 2
    cost = pl.CostEstimate(flops=4 * feat.size, bytes_accessed=feat.size, transcendentals=0)
    part, by_z, kept, by_cell, seen = pl.pallas_call(
        functools.partial(partial_body, n, split),
        in_specs=[smem, hbm, hbm, hbm],
        out_specs=[vmem] * 5,
        out_shape=[
            block,
            jax.ShapeDtypeStruct((tiles, rows * zs, cells), F32),
            jax.ShapeDtypeStruct(feat.shape, BF),
            jax.ShapeDtypeStruct((tiles, cells, rows * zs), BF),
            jax.ShapeDtypeStruct((y_len // chans, zs, chans), F32),
        ],
        scratch_shapes=[pltpu.VMEM(occ.shape, jnp.int32), pltpu.VMEM(hgt.shape, jnp.int32)]
        + wide
        + [pltpu.SemaphoreType.DMA((tiles,)), pltpu.SemaphoreType.DMA((2,))],
        compiler_params=pltpu.CompilerParams(vmem_limit_bytes=16 << 20),
        cost_estimate=cost,
        name="partials",
    )(me.reshape(1), *(pltpu.with_memory_space_constraint(a, pltpu.MemorySpace.HBM) for a in (feat, occ, hgt)))
    if not split:
        return part[part.shape[0] // 2 :], part[: part.shape[0] // 2], by_z, kept
    own = pl.pallas_call(
        functools.partial(own_body, n),
        in_specs=[smem] + [vmem] * 3,
        out_specs=vmem,
        out_shape=block,
        scratch_shapes=wide,
        compiler_params=pltpu.CompilerParams(vmem_limit_bytes=8 << 20),
        cost_estimate=cost,
        name="own_partials",
    )(me.reshape(1), kept, by_cell, seen)
    return part, own, by_z, kept


def pool_body(feat_ref, by_z_ref, xy_ref, xz_ref, xz_acc, xz_cnt):
    rows, _, zs, chans = feat_ref.shape
    _, _, ys, _ = xy_ref.shape
    tiles, _, cells = by_z_ref.shape
    tile_y = cells // zs
    both, group = tile_y + zs, min(ys, tile_y)
    iota = lambda axis: lax.broadcasted_iota(jnp.int32, (tile_y, cells), axis)
    same_y = (iota(0) == iota(1) // zs).astype(F32)
    ones = jnp.ones((cells, chans), BF)
    xz_acc[...] = jnp.zeros_like(xz_acc)
    xz_cnt[...] = jnp.zeros_like(xz_cnt)

    def tile(t, _):
        first = t * tile_y
        picks = []
        for x in range(rows):
            row_z = by_z_ref[t, x * zs : (x + 1) * zs]
            picks += [jnp.sum(row_z, axis=0, keepdims=True) * same_y, row_z]
        picks = jnp.concatenate(picks, axis=0).astype(BF)
        counts = jnp.dot(picks, ones, preferred_element_type=F32)
        for x in range(rows):
            pick = slice(x * both, (x + 1) * both)
            cells_x = feat_ref[x, pl.ds(first, tile_y)].reshape(cells, chans)
            sums = jnp.dot(picks[pick], cells_x, preferred_element_type=F32)
            pool = (sums[:tile_y] * lax.rsqrt(1.0 + counts[pick][:tile_y])).astype(BF)
            for g in range(tile_y // group):
                start = first + g * group
                at = slice(None) if group == ys else pl.ds(pl.multiple_of(start % ys, group), group)
                xy_ref[start // ys, x, at] = pool[g * group : (g + 1) * group]
            xz_acc[x] += sums[tile_y:]
            xz_cnt[x] += counts[pick][tile_y:]

    lax.fori_loop(0, tiles, tile, None)
    xz_ref[...] = (xz_acc[...] * lax.rsqrt(1.0 + xz_cnt[...])).astype(BF)


def pools(feat, by_z, n):
    rows, y_len, zs, chans = feat.shape
    vmem = pl.BlockSpec(memory_space=pltpu.VMEM)
    return pl.pallas_call(
        pool_body,
        in_specs=[vmem] * 2,
        out_specs=[vmem] * 2,
        out_shape=[
            jax.ShapeDtypeStruct((n, rows, y_len // n, chans), BF),
            jax.ShapeDtypeStruct((rows, zs, chans), BF),
        ],
        scratch_shapes=[pltpu.VMEM((rows, zs, chans), F32)] * 2,
        compiler_params=pltpu.CompilerParams(vmem_limit_bytes=8 << 20),
        cost_estimate=pl.CostEstimate(flops=2 * 32 * feat.size, bytes_accessed=1 << 20, transcendentals=0),
        name="pools",
    )(feat, by_z)


def planes_body(xy_ref, xz_ref, xy_in, xy_out, xz_in, xz_out, xy_plane, xz_plane):
    size = min(256, xy_ref.shape[0])
    for r in range(0, xy_ref.shape[0], size):
        xy_plane[r : r + size] = mlp(xy_ref[r : r + size], 0.5 * xy_in[...], xy_out[...])
    xz_plane[...] = mlp(xz_ref[...], 0.5 * xz_in[...], xz_out[...])


def planes(xy_pool, xz_pool, xy_in, xy_out, xz_in, xz_out):
    vmem = pl.BlockSpec(memory_space=pltpu.VMEM)
    flops = 4 * (xy_pool.size + xz_pool.size) * xy_in.shape[1]
    return pl.pallas_call(
        planes_body,
        in_specs=[vmem] * 6,
        out_specs=[vmem] * 2,
        out_shape=[jax.ShapeDtypeStruct(xy_pool.shape, BF), jax.ShapeDtypeStruct(xz_pool.shape, BF)],
        compiler_params=pltpu.CompilerParams(vmem_limit_bytes=8 << 20),
        cost_estimate=pl.CostEstimate(flops=flops, bytes_accessed=1 << 20, transcendentals=0),
        name="planes",
    )(xy_pool, xz_pool, xy_in, xy_out, xz_in, xz_out)


def yz_body(parts, zs, *refs):
    w_in, w_out, out = refs[parts:]
    count, cells, chans = out.shape
    pools = []
    ys = cells // zs
    for u in range(count):
        total, seen = 0.0, 0.0
        for v in range(parts):
            at = (u ^ v) * cells
            total = total + refs[v][0, at : at + cells].astype(F32)
            seen = seen + refs[v][0, count * cells :, (u ^ v) * ys : (u ^ v) * ys + ys].astype(F32)
        scale = lax.rsqrt(1.0 + seen)
        pools += [
            total[y * zs : (y + 1) * zs] * jnp.broadcast_to(scale[:, y : y + 1], (zs, chans)) for y in range(ys)
        ]
    pool = jnp.concatenate(pools, axis=0).astype(BF)
    out[...] = mlp(pool, 0.5 * w_in[...], w_out[...]).reshape(count, cells, chans)


def yz_mlp(parts, zs, w_in, w_out):
    vmem = pl.BlockSpec(memory_space=pltpu.VMEM)
    count, chans = len(parts), parts[0].shape[2]
    cells = (parts[0].shape[1] - zs) // count
    return pl.pallas_call(
        functools.partial(yz_body, len(parts), zs),
        in_specs=[vmem] * (len(parts) + 2),
        out_specs=vmem,
        out_shape=jax.ShapeDtypeStruct((count, cells, chans), BF),
        compiler_params=pltpu.CompilerParams(vmem_limit_bytes=8 << 20),
        cost_estimate=pl.CostEstimate(
            flops=4 * count * cells * w_in.size, bytes_accessed=1 << 19, transcendentals=0
        ),
        name="yz_mlp",
    )(*parts, w_in, w_out)


def first_body(feat_ref, xy_ref, xz_ref, w_in, out_ref):
    n, rows, ys, chans = xy_ref.shape
    zs = xz_ref.shape[1]
    half = 0.5 * w_in[...]

    def chunk(c, _):
        for x in range(rows):
            xy = xy_ref[c, x].astype(F32)
            part = feat_ref[x, pl.ds(c * ys, ys)].astype(F32) + xy[:, None, :] + xz_ref[x].astype(F32)[None]
            part = part.reshape(ys * zs, chans).astype(BF)
            out_ref[c, x] = jnp.dot(part, half, preferred_element_type=F32)

    lax.fori_loop(0, n, chunk, None)


def first_layer(feat, xy_plane, xz_plane, w_in):
    n, rows, ys, _ = xy_plane.shape
    vmem = pl.BlockSpec(memory_space=pltpu.VMEM)
    return pl.pallas_call(
        first_body,
        in_specs=[vmem] * 4,
        out_specs=vmem,
        out_shape=jax.ShapeDtypeStruct((n, rows, ys * xz_plane.shape[1], w_in.shape[1]), F32),
        compiler_params=pltpu.CompilerParams(vmem_limit_bytes=8 << 20),
        cost_estimate=pl.CostEstimate(flops=2 * feat.size * w_in.shape[1], bytes_accessed=1 << 20, transcendentals=0),
        name="first_layer",
    )(feat, xy_plane, xz_plane, w_in)


def voxel_body(n, groups, before, last, me_ref, first_ref, w_in, w_out, *refs):
    yz_refs, refs = refs[: len(groups)], refs[len(groups) :]
    if before:
        prev_ref, refs = refs[0], refs[2:]
    out_hbm, done_ref, own_ref, sems = refs
    _, rows, ys, zs, chans = done_ref.shape
    half = 0.5 * w_in[...]

    def send(source, index, pos, sem):
        at = pl.ds((offset(pos, n) ^ me_ref[0]) * ys, ys)
        return pltpu.make_async_copy(source.at[index], out_hbm.at[:, at], sems.at[sem])

    copies = [send(prev_ref, j, pos, j) for j, pos in enumerate(before)]
    for copy in copies:
        copy.start()
    slot = 0
    for yz_ref, (_, count) in zip(yz_refs, groups):
        both = yz_ref[...].reshape(count * ys * zs, chans)
        both = jnp.dot(both, half, preferred_element_type=F32)
        own_ref[slot : slot + count] = both.reshape(count, ys * zs, half.shape[1])
        slot += count
    slot = 0
    for yz_ref, (pos0, count) in zip(yz_refs, groups):

        def chunk(j, _, yz_ref=yz_ref, pos0=pos0, slot=slot):
            home = offset(pos0 + j, n) ^ me_ref[0]
            for x in range(0, rows, 6):
                hidden = silu((first_ref[home, x : x + 6] + own_ref[slot + j][None]).astype(BF)).astype(BF)
                cells = jnp.dot(hidden.reshape(6 * ys * zs, -1), w_out[...], preferred_element_type=F32).astype(BF)
                done_ref[slot + j, x : x + 6] = cells.reshape(6, ys, zs, chans)
            if last:
                send(done_ref, slot + j, pos0 + j, len(before) + slot + j).start()

        lax.fori_loop(0, count, chunk, None)
        slot += count
    if last:
        slot = 0
        for pos0, count in groups:
            copies += [send(done_ref, slot + j, pos0 + j, len(before) + slot + j) for j in range(count)]
            slot += count
    for copy in copies:
        copy.wait()


def voxels(state, n, groups, yz, last, me, shape, first, w_in, w_out):
    rows, y_len, zs, chans = shape
    ys, size = y_len // n, sum(count for _, count in groups)
    before, extra = ([], []) if state is None else (state[0], list(state[1:]))
    vmem = pl.BlockSpec(memory_space=pltpu.VMEM)
    hbm = pl.BlockSpec(memory_space=pltpu.MemorySpace.HBM)
    done = (size, rows, ys, zs, chans)
    operands = [me.reshape(1), first, w_in, w_out, *yz, *extra]
    sems = pltpu.SemaphoreType.DMA((len(before) + (size if last else 0) or 1,))
    out = pl.pallas_call(
        functools.partial(voxel_body, n, groups, before, last),
        in_specs=[pl.BlockSpec(memory_space=pltpu.SMEM)] + [vmem] * (3 + len(yz)) + [vmem, hbm][: len(extra)],
        out_specs=[hbm] if last else [hbm, vmem],
        out_shape=[jax.ShapeDtypeStruct(shape, BF)] + ([] if last else [jax.ShapeDtypeStruct(done, BF)]),
        scratch_shapes=([pltpu.VMEM(done, BF)] if last else [])
        + [pltpu.VMEM((size, ys * zs, w_in.shape[1]), F32), sems],
        input_output_aliases={len(operands) - 1: 0} if extra else {},
        compiler_params=pltpu.CompilerParams(vmem_limit_bytes=20 << 20, has_side_effects=True),
        cost_estimate=pl.CostEstimate(
            flops=4 * size * rows * ys * zs * w_in.size, bytes_accessed=1 << 20, transcendentals=0
        ),
        name="voxels",
    )(*operands)
    if last:
        return out[0]
    return [pos0 + j for pos0, count in groups for j in range(count)], out[1], out[0]


def swap(value, n, offset):
    return lax.ppermute(value, "gx", [(i, i ^ offset) for i in range(n)])


def per_device(n, features, occupancy, heights, xy_in, xy_out, xz_in, xz_out, yz_in, yz_out, voxel_in, voxel_out):
    zs = features.shape[2]
    me = lax.axis_index("gx")
    theirs, held, by_z, feat = partials(features, jnp.swapaxes(occupancy, 1, 2), heights, me, n)
    chans = features.shape[3]

    digits = radices(n)
    weights = [1]
    for digit in digits:
        weights.append(weights[-1] * digit)
    for stage, digit in enumerate(digits[:-1]):
        size = held.shape[0] // digit
        if stage == 0:
            pieces = [held, swap(theirs, n, 1)]
        else:
            pieces = [held[:size]] + [
                swap(held[d * size : (d + 1) * size], n, mask(d, weights[stage])) for d in range(1, digit)
            ]
        if stage == 1:
            pieces, xy_plane, xz_plane = lax.optimization_barrier((pieces, xy_plane, xz_plane))
        held = sum(piece.astype(F32) for piece in pieces).astype(BF)
        if stage == 0:
            held, by_z = lax.optimization_barrier((held, by_z))
            xy_pool, xz_pool = pools(feat, by_z, n)
            xy_plane, xz_plane = planes(
                xy_pool.reshape(-1, chans), xz_pool.reshape(-1, chans), xy_in, xy_out, xz_in, xz_out
            )
    first = first_layer(feat, xy_plane.reshape(xy_pool.shape), xz_plane.reshape(xz_pool.shape), voxel_in)
    slower = digits[-1]
    assert held.shape[0] == 1
    pieces = [held] + [swap(held, n, mask(d, weights[len(digits) - 1])) for d in range(1, slower)]
    pieces, first = lax.optimization_barrier((pieces, first))
    plane = yz_mlp(pieces, zs, yz_in, yz_out)

    call = functools.partial(voxels, me=me, shape=features.shape, first=first, w_in=voxel_in, w_out=voxel_out)
    sibling = n // 2
    passed = swap(plane, n, 1)
    state = call(None, n, [(0, slower), (sibling, slower)], [plane, passed], False)
    waiting = []
    for stage, digit in reversed(list(enumerate(digits))[1:-1]):
        arrived = []
        for d in range(1, digit):
            arrived.append(swap(plane, n, mask(d, weights[stage])))
        for d, piece in enumerate(arrived, 1):
            piece, *tail = lax.optimization_barrier((piece, *state[1:]))
            state = (state[0], *tail)
            pieces = waiting + [((d * slower, slower), piece)]
            waiting = [((sibling + d * slower, slower), swap(piece, n, 1))]
            state = call(state, n, [g for g, _ in pieces], [p for _, p in pieces], False)
        plane = jnp.concatenate([plane] + arrived, axis=0)
        slower *= digit
    return call(state, n, [g for g, _ in waiting], [p for _, p in waiting], True)


def solution(mesh):
    split = ("group", "gx")
    in_specs = (P(split, None, None, None), P(split, None, None), P(split, None)) + (P(),) * 8
    n = mesh.shape["gx"]

    def body(*args):
        return per_device(n, *args)

    step = jax.shard_map(
        body, mesh=mesh, in_specs=in_specs, out_specs=P(split, None, None, None), check_vma=False
    )
    if len(radices(n)) > 3:
        return step
    return step
```
